32 devices in a mesh: section: 4 (over y, core), tensor: 8 (over z, x).
Axes of the slice: x: 2, y: 2, z: 4, core: 2. Of those that a mesh axis runs over, the one named last changes fastest.
Arguments:
- tokens: bfloat16 [2, 2, 64, 8192], P(None, None, 'tensor'), may hold values from -6 to 6
- norm_gain: bfloat16 [4, 8192], P('section'), may hold values from 0.099609375 to 1.8984375
- w_query: bfloat16 [4, 8192, 8192], P('section', None, 'tensor'), may hold values from -0.0625 to 0.0625
- w_key: bfloat16 [4, 8192, 1024], P('section', None, 'tensor'), may hold values from -0.0625 to 0.0625
- w_value: bfloat16 [4, 8192, 1024], P('section', None, 'tensor'), may hold values from -0.0625 to 0.0625
- w_out: bfloat16 [4, 8192, 8192], P('section', 'tensor'), may hold values from -0.0625 to 0.0625
Outputs:
- section_outputs: bfloat16 [4, 2, 2, 64, 8192], P('section', None, None, 'tensor')
The draws below stay inside these ranges and needn't reach their ends.
All inputs are finite; a program needn't handle non-finite values.
Results may differ from the reference program's by a relative error of at most 0.018.
Values may be sent and summed in bfloat16 or wider, within the bound.
A program may use at most 128 MiB of HBM per device.

```python
import jax
import jax.numpy as jnp
from jax import lax

D = 8192
HEADS = 64
KV_HEADS = 8
HD = 128
MICRO = 2
BLOCKS = 2
BLOCK = 64
LAYERS = 4
N_SECTION = 4
N_TENSOR = 8


def steps_of(key, extent, split, low, top_value):
    factor_of = 1.0
    for position, shards_of in split:
        draws = jax.random.uniform(jax.random.fold_in(jax.random.fold_in(key, 6), position), (shards_of,), jnp.float32, low / len(split), top_value / len(split))
        factor_of = factor_of * jnp.repeat(jnp.exp(draws), extent[position] // shards_of).reshape((-1,) + (1,) * (len(extent) - 1 - position))
    return factor_of


def scatter_about(stream_key, shape, scale, bound, split=(), kind=jnp.bfloat16):
    gain = steps_of(stream_key, shape, split, -0.22, 0.18) if split else 1.0
    drawn = jax.random.normal(stream_key, shape, jnp.float32) * scale * gain
    return jnp.minimum(jnp.maximum(drawn, -bound), bound).astype(kind)


def setup_inputs(seed: int = 0) -> dict:
    key_of = jax.random.split(jax.random.key(seed), 7)
    return {
        "tokens": scatter_about(key_of[0], (MICRO, BLOCKS, BLOCK, D), 1.0, 6.0, ((2, 8),)),
        "norm_gain": jnp.clip(1.0 + 0.18 * jax.random.normal(key_of[1], (LAYERS, D), jnp.float32), 0.099609375, 1.8984375).astype(jnp.bfloat16),
        "w_query": scatter_about(key_of[2], (LAYERS, D, HEADS * HD), D ** -0.5, 0.0625, ((0, 4), (2, 8))),
        "w_key": scatter_about(key_of[3], (LAYERS, D, KV_HEADS * HD), D ** -0.5, 0.0625, ((0, 4), (2, 8))),
        "w_value": scatter_about(key_of[4], (LAYERS, D, KV_HEADS * HD), D ** -0.5, 0.0625, ((0, 4), (2, 8))),
        "w_out": scatter_about(key_of[5], (LAYERS, HEADS * HD, D), D ** -0.5, 0.0625, ((0, 4), (1, 8))),
    }


EPSILON = 1e-05
ROPE_BASE = 500000.0

def rotate(field, positions):
    half_dim = field.shape[-1] // 2
    frequency = ROPE_BASE ** (-(jnp.arange(half_dim, dtype=jnp.float32) * 2.0) / field.shape[-1])
    angles = positions.astype(jnp.float32)[:, None] * frequency[None, :]
    cosine_table = jnp.cos(angles)[:, None, :]
    sine_table = jnp.sin(angles)[:, None, :]
    lower_half = field[..., :half_dim]
    upper_half = field[..., half_dim:]
    return jnp.concatenate([lower_half * cosine_table - upper_half * sine_table, upper_half * cosine_table + lower_half * sine_table], axis=-1)

def normalize(activations, gain_row):
    widened = activations.astype(jnp.float32)
    factor = lax.rsqrt(lax.optimization_barrier(jnp.mean(widened * widened, axis=-1, keepdims=True)) + EPSILON)
    return (widened * factor * gain_row.astype(jnp.float32)).astype(jnp.bfloat16)

def apply_layer(activations, gain_row, query_weight, key_weight, value_weight, out_weight):
    micro_count, seq_len, model_width = activations.shape
    normed = normalize(activations, gain_row)
    flattened = normed.reshape(micro_count * seq_len, model_width)
    queries = jnp.dot(flattened, query_weight, preferred_element_type=jnp.float32).reshape(micro_count, seq_len, HEADS, HD)
    key_rows = jnp.dot(flattened, key_weight, preferred_element_type=jnp.float32).astype(jnp.bfloat16).reshape(micro_count, seq_len, HD, KV_HEADS)
    key_rows = jnp.swapaxes(key_rows, 2, 3)
    value_rows = jnp.dot(flattened, value_weight, preferred_element_type=jnp.float32).astype(jnp.bfloat16).reshape(micro_count, seq_len, HD, KV_HEADS)
    value_rows = jnp.swapaxes(value_rows, 2, 3)
    positions = jnp.arange(seq_len, dtype=jnp.int32)
    queries = rotate(queries, positions).astype(jnp.bfloat16)
    key_rows = rotate(key_rows.astype(jnp.float32), positions).astype(jnp.bfloat16)
    group_size = HEADS // KV_HEADS
    grouped = queries.reshape(micro_count, seq_len, KV_HEADS, group_size, HD)
    visible = positions[None, :] <= positions[:, None]
    score_scale = 1.0 / HD ** 0.5

    def per_head(head_index):
        query_head = grouped[:, :, head_index].astype(jnp.float32)
        key_head = key_rows[:, :, head_index].astype(jnp.float32)
        value_head = value_rows[:, :, head_index].astype(jnp.float32)
        scores = jnp.einsum('mqgd,mkd->mgqk', query_head, key_head) * score_scale
        weights = jnp.where(visible[None, None], jnp.exp(scores), 0.0)
        weights = (weights / lax.optimization_barrier(jnp.sum(weights, axis=-1, keepdims=True))).astype(jnp.bfloat16)
        return jnp.einsum('mgqk,mkd->mqgd', weights.astype(jnp.float32), value_head).astype(jnp.bfloat16)
    context = lax.map(per_head, jnp.arange(KV_HEADS, dtype=jnp.int32))
    context = jnp.moveaxis(context, 0, 2).reshape(micro_count * seq_len, HEADS * HD)
    grouped_ctx = context.reshape(micro_count * seq_len, N_TENSOR, -1)
    grouped_out = out_weight.reshape(N_TENSOR, -1, model_width)

    def add_group(running, group_index):
        partial_value = jnp.dot(grouped_ctx[:, group_index], grouped_out[group_index], preferred_element_type=jnp.float32).astype(jnp.bfloat16)
        partial_value = lax.optimization_barrier(partial_value)
        return (running + partial_value.astype(jnp.float32), None)
    running, unused = lax.scan(add_group, jnp.zeros((micro_count * seq_len, model_width), jnp.float32), jnp.arange(N_TENSOR, dtype=jnp.int32))
    summed = activations.reshape(micro_count * seq_len, model_width).astype(jnp.float32) + running
    return summed.astype(jnp.bfloat16).reshape(micro_count, seq_len, model_width)

def reference(tokens, norm_gain, w_query, w_key, w_value, w_out):
    micro_count, block_count, block_len, model_width = tokens.shape
    present = tokens.reshape(micro_count, block_count * block_len, model_width)
    results = []
    for layer_index in range(N_SECTION):
        present = apply_layer(present, norm_gain[layer_index], w_query[layer_index], w_key[layer_index], w_value[layer_index], w_out[layer_index])
        results.append(present.reshape(micro_count, block_count, block_len, model_width))
    return jnp.stack(results)
```

```python
import functools
import math

import jax
import jax.numpy as jnp
import numpy as np
from jax import lax
from jax.experimental import pallas as pl
from jax.experimental.pallas import tpu as pltpu
from jax.sharding import PartitionSpec as P

HEADS = 64
KV_HEADS = 8
HD = 128


EPSILON = 1e-05
ROPE_BASE = 500000.0


def shifted(block, axis, distance):
    devices = range(lax.axis_size(axis))
    route = [(i - distance, i) for i in devices if i - distance in devices]
    return lax.ppermute(block, axis, route)


def rotate(field, positions):
    half_dim = field.shape[-1] // 2
    frequency = ROPE_BASE ** (-(jnp.arange(half_dim, dtype=jnp.float32) * 2.0) / field.shape[-1])
    angles = positions.astype(jnp.float32)[:, None] * frequency[None, :]
    cosine_table = jnp.cos(angles)[:, None, :]
    sine_table = jnp.sin(angles)[:, None, :]
    lower_half = field[..., :half_dim]
    upper_half = field[..., half_dim:]
    return jnp.concatenate(
        [
            lower_half * cosine_table - upper_half * sine_table,
            upper_half * cosine_table + lower_half * sine_table,
        ],
        axis=-1,
    )


def normalize(activations, gain_row):
    widened = activations.astype(jnp.float32)
    factor = lax.rsqrt(jnp.mean(widened * widened, axis=-1, keepdims=True) + EPSILON)
    return (widened * factor * gain_row.astype(jnp.float32)).astype(jnp.bfloat16)


def general_body(tokens, norm_gain, w_query, w_key, w_value, w_out):
    section_count = lax.axis_size("section")
    section_index = lax.axis_index("section")
    lane_count = lax.axis_size("tensor")
    lane_index = lax.axis_index("tensor")
    micro_count, block_count, shard_rows, model_width = tokens.shape
    block_len = shard_rows * lane_count
    seq_len = block_count * block_len
    unit_count = micro_count * block_count
    tick_count = unit_count + section_count - 1
    gain_row = norm_gain[0]
    w_joined = jnp.concatenate([w_query[0], w_key[0], w_value[0]], axis=1)
    w_down = w_out[0]
    query_cols = w_query.shape[2]
    key_cols = w_key.shape[2]
    local_heads = query_cols // HD
    kv_index = lane_index * local_heads // (HEADS // KV_HEADS)
    score_scale = 1.0 / math.sqrt(HD)
    offsets = jnp.arange(block_len, dtype=jnp.int32)
    key_positions = jnp.arange(seq_len, dtype=jnp.int32)
    incoming = jnp.zeros((shard_rows, model_width), jnp.bfloat16)
    key_cache = jnp.zeros((micro_count, seq_len, HD), jnp.bfloat16)
    value_cache = jnp.zeros((micro_count, seq_len, HD), jnp.bfloat16)
    stored = jnp.zeros((micro_count, block_count, shard_rows, model_width), jnp.bfloat16)

    def attend(projected, batch_index, block_index, key_cache, value_cache):
        queries = projected[:, :query_cols].reshape(block_len, local_heads, HD)
        key_value = projected[:, query_cols:].astype(jnp.bfloat16)
        gathered = lax.all_gather(key_value, "tensor", axis=1, tiled=True)
        gathered = gathered.reshape(block_len, lane_count, 2, key_cols)
        keys_all = gathered[:, :, 0, :].reshape(block_len, HD, KV_HEADS)
        values_all = gathered[:, :, 1, :].reshape(block_len, HD, KV_HEADS)
        key_new = lax.dynamic_index_in_dim(keys_all, kv_index, 2, keepdims=False)
        value_new = lax.dynamic_index_in_dim(values_all, kv_index, 2, keepdims=False)
        positions = block_index * block_len + offsets
        queries = rotate(queries, positions).astype(jnp.bfloat16)
        key_new = rotate(key_new.astype(jnp.float32)[:, None, :], positions)[:, 0, :].astype(
            jnp.bfloat16
        )
        key_cache = lax.dynamic_update_slice(
            key_cache, key_new[None], (batch_index, block_index * block_len, 0)
        )
        value_cache = lax.dynamic_update_slice(
            value_cache, value_new[None], (batch_index, block_index * block_len, 0)
        )
        key_rows = lax.dynamic_index_in_dim(key_cache, batch_index, 0, keepdims=False)
        value_rows = lax.dynamic_index_in_dim(value_cache, batch_index, 0, keepdims=False)
        scores = (
            jnp.einsum("qhd,kd->hqk", queries, key_rows, preferred_element_type=jnp.float32)
            * score_scale
        )
        visible = key_positions[None, :] <= positions[:, None]
        weights = jnp.where(visible[None], jnp.exp(scores), 0.0)
        weights = (weights / jnp.sum(weights, axis=-1, keepdims=True)).astype(jnp.bfloat16)
        context = jnp.einsum("hqk,kd->qhd", weights, value_rows, preferred_element_type=jnp.float32)
        context = context.astype(jnp.bfloat16).reshape(block_len, query_cols)
        reduced = lax.psum_scatter(
            jnp.dot(context, w_down, preferred_element_type=jnp.float32).astype(jnp.bfloat16),
            "tensor",
            scatter_dimension=0,
            tiled=True,
        ).astype(jnp.float32)
        return (reduced, key_cache, value_cache)

    def advance(tick_index, state_tuple):
        incoming, key_cache, value_cache, stored = state_tuple
        unit_index = tick_index - section_index
        usable = (unit_index >= 0) & (unit_index < unit_count)
        unit_index = jnp.clip(unit_index, 0, unit_count - 1)
        batch_index = unit_index // block_count
        block_index = unit_index % block_count
        arriving = lax.dynamic_slice(
            tokens, (batch_index, block_index, 0, 0), (1, 1, incoming.shape[0], model_width)
        )[0, 0]
        present = jnp.where(section_index == 0, arriving, incoming)
        projected = jnp.dot(
            lax.all_gather(normalize(present, gain_row), "tensor", axis=0, tiled=True),
            w_joined,
            preferred_element_type=jnp.float32,
        )
        reduced, key_cache, value_cache = attend(
            projected, batch_index, block_index, key_cache, value_cache
        )
        result = (present.astype(jnp.float32) + reduced).astype(jnp.bfloat16)
        previous = lax.dynamic_slice(
            stored, (batch_index, block_index, 0, 0), (1, 1, shard_rows, model_width)
        )[0, 0]
        chosen = jnp.where(usable, result, previous)
        stored = lax.dynamic_update_slice(
            stored, chosen[None, None], (batch_index, block_index, 0, 0)
        )
        incoming = shifted(result, "section", 1)
        return (incoming, key_cache, value_cache, stored)

    final_state = lax.fori_loop(0, tick_count, advance, (incoming, key_cache, value_cache, stored))
    return final_state[3][None]


PAIR = 2
MESH = pl.DeviceIdType.MESH


def layer_kernel(
    dims,
    tokens,
    gain_row,
    cos_rows,
    sin_rows,
    cos_cols,
    sin_cols,
    regroup,
    wq_hbm,
    wk_hbm,
    wv_hbm,
    wo_hbm,
    out,
    wq,
    wkv,
    wo,
    gathered,
    normed,
    squares,
    projected,
    queries,
    context,
    kv_send,
    kv_land,
    key_cache,
    value_cache,
    partial,
    pair_land,
    column_sum,
    column_land,
    finished,
    weight_sem,
    own_sem,
    rows_send,
    rows_recv,
    relay_send,
    relay_recv,
    kv_send_sem,
    kv_recv_sem,
    pair_send,
    pair_recv,
    column_send,
    column_recv,
):
    sections, lanes, micro_count, block_count, rows, width, chunks, query_cols = dims
    columns = lanes // PAIR
    units = micro_count * block_count
    chunk = width // chunks
    block_len = rows * lanes
    seq_len = block_count * block_len
    heads = query_cols // HD
    section = lax.axis_index("section")
    lane = lax.axis_index("tensor")
    column = lane // PAIR
    side = lane % PAIR
    other = 1 - side
    partner = column * PAIR + other
    score_scale = 1.0 / math.sqrt(HD)

    def input_weights(c):
        band = pl.ds(c * chunk, chunk)
        return [
            pltpu.make_async_copy(
                wk_hbm.at[0, band], wkv.at[band, pl.ds(0, HD)], weight_sem.at[0, c]
            ),
            pltpu.make_async_copy(
                wv_hbm.at[0, band], wkv.at[band, pl.ds(HD, HD)], weight_sem.at[1, c]
            ),
            pltpu.make_async_copy(wq_hbm.at[0, band], wq.at[band], weight_sem.at[2, c]),
        ]

    output_weights = pltpu.make_async_copy(wo_hbm.at[0], wo, weight_sem.at[3, 0])
    for c in range(chunks):
        for copy in input_weights(c):
            copy.start()
    output_weights.start()

    barrier = pltpu.get_barrier_semaphore()

    def greet(to_section, to_lane):
        pl.semaphore_signal(barrier, inc=1, device_id=(to_section, to_lane), device_id_type=MESH)

    for step in range(1, lanes):
        greet(section, (lane + step) % lanes)

    @pl.when(section > 0)
    def _():
        for z in range(columns):
            greet(section - 1, z * PAIR + side)

    @pl.when(section < sections - 1)
    def _():
        for z in range(columns):
            greet(section + 1, z * PAIR + side)

    neighbours = jnp.minimum(section, 1) + jnp.minimum(sections - 1 - section, 1)
    pl.semaphore_wait(barrier, lanes - 1 + columns * neighbours)

    def rows_copy(source, unit, c, step, to_section):
        to_column = (column + step) % columns
        return pltpu.make_async_remote_copy(
            src_ref=source,
            dst_ref=gathered.at[unit, c, side, column],
            send_sem=rows_send.at[unit, c, step],
            recv_sem=rows_recv.at[unit, c, column],
            device_id=(to_section, to_column * PAIR + side),
            device_id_type=MESH,
        )

    def relay_copy(unit, c, which):
        return pltpu.make_async_remote_copy(
            src_ref=gathered.at[unit, c, which],
            dst_ref=gathered.at[unit, c, which],
            send_sem=relay_send.at[unit, c],
            recv_sem=relay_recv.at[unit, c],
            device_id=(section, partner),
            device_id_type=MESH,
        )

    def kv_copy(unit, step, landing):
        to_lane = (lane + step) % lanes
        return pltpu.make_async_remote_copy(
            src_ref=kv_send.at[unit, to_lane],
            dst_ref=kv_land.at[unit, landing],
            send_sem=kv_send_sem.at[unit, step],
            recv_sem=kv_recv_sem.at[unit, step],
            device_id=(section, to_lane),
            device_id_type=MESH,
        )

    def pair_copy(unit, c):
        return pltpu.make_async_remote_copy(
            src_ref=partial.at[unit, c, other],
            dst_ref=pair_land.at[unit, c],
            send_sem=pair_send.at[unit, c],
            recv_sem=pair_recv.at[unit, c],
            device_id=(section, partner),
            device_id_type=MESH,
        )

    def column_copy(unit, c, step):
        to_column = (column + step) % columns
        return pltpu.make_async_remote_copy(
            src_ref=column_sum.at[unit, c, to_column],
            dst_ref=column_land.at[unit, c, step],
            send_sem=column_send.at[unit, c, step],
            recv_sem=column_recv.at[unit, c, step],
            device_id=(section, to_column * PAIR + side),
            device_id_type=MESH,
        )

    def token_rows(unit, c):
        return tokens.at[unit // block_count, unit % block_count, :, pl.ds(c * chunk, chunk)]

    @pl.when(section == 0)
    def _():
        @pl.loop(0, units)
        def _(unit):
            for c in range(chunks):
                for step in range(1, columns):
                    rows_copy(token_rows(unit, c), unit, c, step, section).start()
                pltpu.make_async_copy(
                    token_rows(unit, c),
                    gathered.at[unit, c, side, column],
                    own_sem.at[unit, c],
                ).start()

    key_cache[...] = jnp.zeros_like(key_cache)
    value_cache[...] = jnp.zeros_like(value_cache)

    def receive(unit, c):
        for step in range(1, columns):
            from_column = (column + step) % columns
            pltpu.make_async_remote_copy(
                src_ref=gathered.at[unit, c, side, from_column],
                dst_ref=gathered.at[unit, c, side, from_column],
                send_sem=rows_send.at[unit, c, step],
                recv_sem=rows_recv.at[unit, c, from_column],
                device_id=(section, partner),
                device_id_type=MESH,
            ).wait_recv()

        @pl.when(section == 0)
        def _():
            pltpu.make_async_copy(
                token_rows(unit, c),
                gathered.at[unit, c, side, column],
                own_sem.at[unit, c],
            ).wait()

        @pl.when(section > 0)
        def _():
            rows_copy(finished.at[unit, c], unit, c, 0, section - 1).wait_recv()

        relay_copy(unit, c, side).start()

    def absorb(unit, c):
        relay_copy(unit, c, other).wait_recv()
        cols = pl.ds(c * chunk, chunk)
        gain = gain_row[:, cols].astype(jnp.float32)
        for z in range(columns):
            band = slice(z * PAIR * rows, (z + 1) * PAIR * rows)
            x = jnp.concatenate(
                [gathered[unit, c, i, z].astype(jnp.float32) for i in range(PAIR)], axis=0
            )
            square = jnp.sum(x * x, axis=-1, keepdims=True)
            if c == 0:
                squares[band, :] = jnp.broadcast_to(square, (PAIR * rows, HD))
            else:
                squares[band, :] += square
            normed[band, :] = (x * gain).astype(jnp.bfloat16)
        product = jnp.dot(normed[...], wkv[cols, :], preferred_element_type=jnp.float32)
        if c == 0:
            projected[:, pl.ds(query_cols, 2 * HD)] = product
        else:
            projected[:, pl.ds(query_cols, 2 * HD)] += product

    def absorb_queries(c):
        @pl.loop(0, query_cols // SPAN)
        def _(part):
            place = pl.ds(pl.multiple_of(part * SPAN, SPAN), SPAN)
            product = jnp.dot(
                normed[...],
                wq[pl.ds(c * chunk, chunk), place],
                preferred_element_type=jnp.float32,
            )
            if c == 0:
                projected[:, place] = product
            else:
                projected[:, place] += product

    def row_factor():
        return lax.rsqrt(squares[:, :1] * (1.0 / width) + EPSILON)

    def share_keys(unit):
        key_value = projected[:, pl.ds(query_cols, 2 * HD)] * row_factor()
        stacked = jnp.concatenate([key_value[:, :HD], key_value[:, HD:]], axis=0)
        turned = lax.dot_general(
            regroup[...],
            stacked.astype(jnp.bfloat16),
            (((1,), (1,)), ((), ())),
            preferred_element_type=jnp.float32,
        ).astype(jnp.bfloat16)
        kv_send[unit] = turned.reshape(lanes, HD // lanes, 2 * block_len)
        for step in range(1, lanes):
            kv_copy(unit, step, lane).start()
        kv_land[unit, lane] = kv_send[unit, lane]

    def attend(unit):
        micro = unit // block_count
        block = unit % block_count
        factor = row_factor()
        cosine = cos_rows[block]
        sine = sin_rows[block]
        for h in range(heads):
            head = projected[:, pl.ds(h * HD, HD)] * factor
            turned_head = head * cosine + pltpu.roll(head, HD // 2, 1) * sine
            queries[pl.ds(h * block_len, block_len), :] = turned_head.astype(jnp.bfloat16)

        for step in range(1, lanes):
            kv_copy(unit, step, (lane + lanes - step) % lanes).wait_recv()
        landed = kv_land[unit].reshape(HD, 2 * block_len).astype(jnp.float32)
        lower = landed[: HD // 2]
        upper = landed[HD // 2 :]
        cosine_col = cos_cols[block]
        sine_col = sin_cols[block]
        rotated = jnp.concatenate(
            [lower * cosine_col - upper * sine_col, upper * cosine_col + lower * sine_col], axis=0
        )
        place = lax.broadcasted_iota(jnp.int32, (HD, seq_len), 1)
        fresh = place // block_len == block
        swapped = jnp.where(block == 0, rotated, pltpu.roll(rotated, block_len, 1))
        keys = jnp.where(fresh, swapped, key_cache[micro].astype(jnp.float32)).astype(jnp.bfloat16)
        key_cache[micro] = keys
        swapped = jnp.where(block == 0, pltpu.roll(landed, block_len, 1), landed)
        values = jnp.where(fresh, swapped, value_cache[micro].astype(jnp.float32)).astype(
            jnp.bfloat16
        )
        value_cache[micro] = values

        stack = heads * block_len
        position = (
            lax.broadcasted_iota(jnp.int32, (stack, seq_len), 0) % block_len + block * block_len
        )
        key_position = lax.broadcasted_iota(jnp.int32, (stack, seq_len), 1)
        scores = jnp.dot(queries[...], keys, preferred_element_type=jnp.float32) * score_scale
        piece = jnp.where(key_position <= position, jnp.exp(scores), 0.0)
        denominator = jnp.sum(piece, axis=-1, keepdims=True)
        result = lax.dot_general(
            (piece / denominator).astype(jnp.bfloat16),
            values,
            (((1,), (1,)), ((), ())),
            preferred_element_type=jnp.float32,
        ).astype(jnp.bfloat16)
        for h in range(heads):
            context[:, pl.ds(h * HD, HD)] = result[h * block_len : (h + 1) * block_len]

    def down(unit, c):
        tile = TILE

        @pl.loop(0, chunk // tile)
        def _(n):
            start = pl.multiple_of(n * tile, tile)
            product = jnp.dot(
                context[...],
                wo[:, pl.ds(pl.multiple_of(c * chunk + start, tile), tile)],
                preferred_element_type=jnp.float32,
            )
            blocks = product.reshape(columns, PAIR, rows, tile).astype(jnp.bfloat16)
            for i in range(PAIR):
                partial[unit, c, i, :, :, pl.ds(start, tile)] = blocks[:, i]

        pair_copy(unit, c).start()

    def add_pair(unit, c):
        pair_copy(unit, c).wait_recv()
        for z in range(columns):
            column_sum[unit, c, z] = (
                partial[unit, c, side, z].astype(jnp.float32)
                + pair_land[unit, c, z].astype(jnp.float32)
            ).astype(jnp.bfloat16)
        for step in range(1, columns):
            column_copy(unit, c, step).start()

    def finish(unit, c):
        total = gathered[unit, c, side, column].astype(jnp.float32)
        total = total + column_sum[unit, c, column].astype(jnp.float32)
        for step in range(1, columns):
            column_copy(unit, c, step).wait_recv()
            total = total + column_land[unit, c, step].astype(jnp.float32)
        result = total.astype(jnp.bfloat16)
        finished[unit, c] = result
        out[0, unit // block_count, unit % block_count, :, pl.ds(c * chunk, chunk)] = result

        @pl.when(section < sections - 1)
        def _():
            for step in range(columns):
                rows_copy(finished.at[unit, c], unit, c, step, section + 1).start()

    @pl.when(section == 0)
    def _():
        for c in range(chunks):
            receive(0, c)

    @pl.loop(0, units + 1)
    def _(turn):
        older = turn - 1

        def step_of(name, c):
            if name == "D":
                down(older, c)
            elif name == "P":
                add_pair(older, c)
            elif name == "F":
                finish(older, c)
            elif name == "R":
                @pl.when(section > 0)
                def _():
                    receive(turn, c)
            elif name == "E":
                @pl.when((section == 0) & (turn < units - 1))
                def _():
                    receive(turn + 1, c)
            elif name == "A":

                @pl.when(turn == 0)
                def _():
                    for copy in input_weights(c):
                        copy.wait()

                absorb(turn, c)
                if c < chunks - 1:
                    absorb_queries(c)
            elif name == "K":
                share_keys(turn)
                absorb_queries(chunks - 1)
            elif name == "T":
                attend(turn)

                @pl.when(turn == 0)
                def _():
                    output_weights.wait()

        groups = []
        for word in SCHEDULE:
            late = word[0] in "DPF"
            if not groups or groups[-1][0] != late:
                groups.append((late, []))
            groups[-1][1].append((word[0], int(word[1:] or 0)))
        for late, members in groups:
            @pl.when((turn > 0) if late else (turn < units))
            def _():
                for name, c in members:
                    step_of(name, c)

    @pl.loop(0, units)
    def _(unit):
        for c in range(chunks):
            relay_copy(unit, c, side).wait_send()
            pair_copy(unit, c).wait_send()
            for step in range(1, columns):
                column_copy(unit, c, step).wait_send()
        for step in range(1, lanes):
            kv_copy(unit, step, lane).wait_send()

    @pl.when(section == 0)
    def _():
        @pl.loop(0, units)
        def _(unit):
            for c in range(chunks):
                for step in range(1, columns):
                    rows_copy(token_rows(unit, c), unit, c, step, section).wait_send()

    @pl.when(section < sections - 1)
    def _():
        @pl.loop(0, units)
        def _(unit):
            for c in range(chunks):
                for step in range(columns):
                    rows_copy(finished.at[unit, c], unit, c, step, section + 1).wait_send()


def kernel_body(tokens, norm_gain, w_query, w_key, w_value, w_out):
    sections = lax.axis_size("section")
    lanes = lax.axis_size("tensor")
    micro_count, block_count, rows, width = tokens.shape
    query_cols = w_query.shape[2]
    block_len = rows * lanes
    seq_len = block_count * block_len
    units = micro_count * block_count
    columns = lanes // PAIR
    chunks = CHUNKS
    chunk = width // chunks
    half = HD // 2
    frequency = np.power(
        np.float32(ROPE_BASE), -(np.arange(half, dtype=np.float32) * np.float32(2.0)) / np.float32(HD)
    )
    angles = np.arange(seq_len, dtype=np.float32)[:, None] * frequency[None, :]
    cosine, sine = np.cos(angles), np.sin(angles)
    cos_rows = np.concatenate([cosine, cosine], axis=1).reshape(block_count, block_len, HD)
    sin_rows = np.concatenate([-sine, sine], axis=1).reshape(block_count, block_len, HD)

    def by_column(table):
        table = np.swapaxes(table.reshape(block_count, block_len, half), 1, 2)
        return np.concatenate([table, table], axis=2)

    entries = HD // KV_HEADS
    target = np.arange(HD)
    source = (target % entries) * KV_HEADS + target // entries
    regroup = (source[:, None] == np.arange(HD)[None, :]).astype(jnp.bfloat16)
    dims = (sections, lanes, micro_count, block_count, rows, width, chunks, query_cols)
    vmem = pl.BlockSpec(memory_space=pltpu.VMEM)
    hbm = pl.BlockSpec(memory_space=pl.ANY)
    dma = pltpu.SemaphoreType.DMA
    bf16 = jnp.bfloat16
    return pl.pallas_call(
        functools.partial(layer_kernel, dims),
        out_shape=jax.ShapeDtypeStruct((1,) + tokens.shape, bf16),
        in_specs=[vmem] * 7 + [hbm] * 4,
        out_specs=vmem,
        scratch_shapes=[
            pltpu.VMEM((width, query_cols), bf16),
            pltpu.VMEM((width, 2 * HD), bf16),
            pltpu.VMEM((query_cols, width), bf16),
            pltpu.VMEM((units, chunks, PAIR, columns, rows, chunk), bf16),
            pltpu.VMEM((block_len, chunk), bf16),
            pltpu.VMEM((block_len, HD), jnp.float32),
            pltpu.VMEM((block_len, query_cols + 2 * HD), jnp.float32),
            pltpu.VMEM((query_cols // HD * block_len, HD), bf16),
            pltpu.VMEM((block_len, query_cols), bf16),
            pltpu.VMEM((units, lanes, HD // lanes, 2 * block_len), bf16),
            pltpu.VMEM((units, lanes, HD // lanes, 2 * block_len), bf16),
            pltpu.VMEM((micro_count, HD, seq_len), bf16),
            pltpu.VMEM((micro_count, HD, seq_len), bf16),
            pltpu.VMEM((units, chunks, PAIR, columns, rows, chunk), bf16),
            pltpu.VMEM((units, chunks, columns, rows, chunk), bf16),
            pltpu.VMEM((units, chunks, columns, rows, chunk), bf16),
            pltpu.VMEM((units, chunks, columns, rows, chunk), bf16),
            pltpu.VMEM((units, chunks, rows, chunk), bf16),
            dma((4, chunks)),
            dma((units, chunks)),
            dma((units, chunks, columns)),
            dma((units, chunks, columns)),
            dma((units, chunks)),
            dma((units, chunks)),
            dma((units, lanes)),
            dma((units, lanes)),
            dma((units, chunks)),
            dma((units, chunks)),
            dma((units, chunks, columns)),
            dma((units, chunks, columns)),
        ],
        compiler_params=pltpu.CompilerParams(
            collective_id=0, has_side_effects=True, vmem_limit_bytes=67043328
        ),
    )(
        tokens,
        norm_gain,
        jnp.asarray(cos_rows),
        jnp.asarray(sin_rows),
        jnp.asarray(by_column(cosine)),
        jnp.asarray(by_column(sine)),
        jnp.asarray(regroup),
        w_query,
        w_key,
        w_value,
        w_out,
    )


CHUNKS = 4
SPAN = 1024
TILE = 2048
SCHEDULE = ("D0", "D1", "D2", "D3", "P0", "P1", "E0", "E1", "R0", "P2", "R1", "P3", "R2", "E2", "E3", "F0", "R3", "A0", "F1", "A1", "F2", "A2", "F3", "A3", "K", "T")


def body(tokens, norm_gain, w_query, w_key, w_value, w_out):
    lanes = lax.axis_size("tensor")
    fits = (
        lanes == KV_HEADS
        and w_key.shape[2] == HD
        and w_query.shape[2] == HEADS // KV_HEADS * HD
        and tokens.shape[2] == 8
        and tokens.shape[2] * lanes * 2 == HD
        and tokens.shape[1] == 2
        and tokens.shape[3] % (CHUNKS * TILE) == 0
        and w_query.shape[2] % SPAN == 0
    )
    chosen = kernel_body if fits else general_body
    return chosen(tokens, norm_gain, w_query, w_key, w_value, w_out)


def solution(mesh):
    return jax.shard_map(
        body,
        mesh=mesh,
        in_specs=(
            P(None, None, "tensor", None),
            P("section", None),
            P("section", None, "tensor"),
            P("section", None, "tensor"),
            P("section", None, "tensor"),
            P("section", "tensor", None),
        ),
        out_specs=P("section", None, None, "tensor", None),
        check_vma=False,
    )
```

```python
import functools
import math

import jax
import jax.numpy as jnp
import numpy as np
from jax import lax
from jax.experimental import pallas as pl
from jax.experimental.pallas import tpu as pltpu
from jax.sharding import PartitionSpec as P

HEADS = 64
KV_HEADS = 8
HD = 128


EPSILON = 1e-05
ROPE_BASE = 500000.0


def shifted(block, axis, distance):
    devices = range(lax.axis_size(axis))
    route = [(i - distance, i) for i in devices if i - distance in devices]
    return lax.ppermute(block, axis, route)


def rotate(field, positions):
    half_dim = field.shape[-1] // 2
    frequency = ROPE_BASE ** (-(jnp.arange(half_dim, dtype=jnp.float32) * 2.0) / field.shape[-1])
    angles = positions.astype(jnp.float32)[:, None] * frequency[None, :]
    cosine_table = jnp.cos(angles)[:, None, :]
    sine_table = jnp.sin(angles)[:, None, :]
    lower_half = field[..., :half_dim]
    upper_half = field[..., half_dim:]
    return jnp.concatenate(
        [
            lower_half * cosine_table - upper_half * sine_table,
            upper_half * cosine_table + lower_half * sine_table,
        ],
        axis=-1,
    )


def normalize(activations, gain_row):
    widened = activations.astype(jnp.float32)
    factor = lax.rsqrt(jnp.mean(widened * widened, axis=-1, keepdims=True) + EPSILON)
    return (widened * factor * gain_row.astype(jnp.float32)).astype(jnp.bfloat16)


def general_body(tokens, norm_gain, w_query, w_key, w_value, w_out):
    section_count = lax.axis_size("section")
    section_index = lax.axis_index("section")
    lane_count = lax.axis_size("tensor")
    lane_index = lax.axis_index("tensor")
    micro_count, block_count, shard_rows, model_width = tokens.shape
    block_len = shard_rows * lane_count
    seq_len = block_count * block_len
    unit_count = micro_count * block_count
    tick_count = unit_count + section_count - 1
    gain_row = norm_gain[0]
    w_joined = jnp.concatenate([w_query[0], w_key[0], w_value[0]], axis=1)
    w_down = w_out[0]
    query_cols = w_query.shape[2]
    key_cols = w_key.shape[2]
    local_heads = query_cols // HD
    kv_index = lane_index * local_heads // (HEADS // KV_HEADS)
    score_scale = 1.0 / math.sqrt(HD)
    offsets = jnp.arange(block_len, dtype=jnp.int32)
    key_positions = jnp.arange(seq_len, dtype=jnp.int32)
    incoming = jnp.zeros((shard_rows, model_width), jnp.bfloat16)
    key_cache = jnp.zeros((micro_count, seq_len, HD), jnp.bfloat16)
    value_cache = jnp.zeros((micro_count, seq_len, HD), jnp.bfloat16)
    stored = jnp.zeros((micro_count, block_count, shard_rows, model_width), jnp.bfloat16)

    def attend(projected, batch_index, block_index, key_cache, value_cache):
        queries = projected[:, :query_cols].reshape(block_len, local_heads, HD)
        key_value = projected[:, query_cols:].astype(jnp.bfloat16)
        gathered = lax.all_gather(key_value, "tensor", axis=1, tiled=True)
        gathered = gathered.reshape(block_len, lane_count, 2, key_cols)
        keys_all = gathered[:, :, 0, :].reshape(block_len, HD, KV_HEADS)
        values_all = gathered[:, :, 1, :].reshape(block_len, HD, KV_HEADS)
        key_new = lax.dynamic_index_in_dim(keys_all, kv_index, 2, keepdims=False)
        value_new = lax.dynamic_index_in_dim(values_all, kv_index, 2, keepdims=False)
        positions = block_index * block_len + offsets
        queries = rotate(queries, positions).astype(jnp.bfloat16)
        key_new = rotate(key_new.astype(jnp.float32)[:, None, :], positions)[:, 0, :].astype(
            jnp.bfloat16
        )
        key_cache = lax.dynamic_update_slice(
            key_cache, key_new[None], (batch_index, block_index * block_len, 0)
        )
        value_cache = lax.dynamic_update_slice(
            value_cache, value_new[None], (batch_index, block_index * block_len, 0)
        )
        key_rows = lax.dynamic_index_in_dim(key_cache, batch_index, 0, keepdims=False)
        value_rows = lax.dynamic_index_in_dim(value_cache, batch_index, 0, keepdims=False)
        scores = (
            jnp.einsum("qhd,kd->hqk", queries, key_rows, preferred_element_type=jnp.float32)
            * score_scale
        )
        visible = key_positions[None, :] <= positions[:, None]
        weights = jnp.where(visible[None], jnp.exp(scores), 0.0)
        weights = (weights / jnp.sum(weights, axis=-1, keepdims=True)).astype(jnp.bfloat16)
        context = jnp.einsum("hqk,kd->qhd", weights, value_rows, preferred_element_type=jnp.float32)
        context = context.astype(jnp.bfloat16).reshape(block_len, query_cols)
        reduced = lax.psum_scatter(
            jnp.dot(context, w_down, preferred_element_type=jnp.float32).astype(jnp.bfloat16),
            "tensor",
            scatter_dimension=0,
            tiled=True,
        ).astype(jnp.float32)
        return (reduced, key_cache, value_cache)

    def advance(tick_index, state_tuple):
        incoming, key_cache, value_cache, stored = state_tuple
        unit_index = tick_index - section_index
        usable = (unit_index >= 0) & (unit_index < unit_count)
        unit_index = jnp.clip(unit_index, 0, unit_count - 1)
        batch_index = unit_index // block_count
        block_index = unit_index % block_count
        arriving = lax.dynamic_slice(
            tokens, (batch_index, block_index, 0, 0), (1, 1, incoming.shape[0], model_width)
        )[0, 0]
        present = jnp.where(section_index == 0, arriving, incoming)
        projected = jnp.dot(
            lax.all_gather(normalize(present, gain_row), "tensor", axis=0, tiled=True),
            w_joined,
            preferred_element_type=jnp.float32,
        )
        reduced, key_cache, value_cache = attend(
            projected, batch_index, block_index, key_cache, value_cache
        )
        result = (present.astype(jnp.float32) + reduced).astype(jnp.bfloat16)
        previous = lax.dynamic_slice(
            stored, (batch_index, block_index, 0, 0), (1, 1, shard_rows, model_width)
        )[0, 0]
        chosen = jnp.where(usable, result, previous)
        stored = lax.dynamic_update_slice(
            stored, chosen[None, None], (batch_index, block_index, 0, 0)
        )
        incoming = shifted(result, "section", 1)
        return (incoming, key_cache, value_cache, stored)

    final_state = lax.fori_loop(0, tick_count, advance, (incoming, key_cache, value_cache, stored))
    return final_state[3][None]


PAIR = 2
MESH = pl.DeviceIdType.MESH


def layer_kernel(
    dims,
    tokens,
    gain_row,
    cos_rows,
    sin_rows,
    cos_cols,
    sin_cols,
    regroup,
    wq_hbm,
    wk_hbm,
    wv_hbm,
    wo_hbm,
    out,
    wq,
    wkv,
    wo,
    gathered,
    normed,
    squares,
    projected,
    queries,
    context,
    kv_send,
    kv_land,
    key_cache,
    value_cache,
    partial,
    pair_land,
    column_sum,
    column_land,
    finished,
    weight_sem,
    own_sem,
    rows_send,
    rows_recv,
    relay_send,
    relay_recv,
    kv_send_sem,
    kv_recv_sem,
    pair_send,
    pair_recv,
    column_send,
    column_recv,
    mixer,
    trade_send,
    trade_land,
    trade_send_sem,
    trade_recv_sem,
):
    sections, lanes, micro_count, block_count, rows, width, chunks, query_cols = dims
    columns = lanes // PAIR
    units = micro_count * block_count
    chunk = width // chunks
    block_len = rows * lanes
    seq_len = block_count * block_len
    heads = query_cols // HD
    section = lax.axis_index("section")
    lane = lax.axis_index("tensor")
    column = lane // PAIR
    side = lane % PAIR
    other = 1 - side
    partner = column * PAIR + other
    score_scale = 1.0 / math.sqrt(HD)

    def shared_weights(c):
        band = pl.ds(c * chunk, chunk)
        return [
            pltpu.make_async_copy(
                wk_hbm.at[0, band], wkv.at[band, pl.ds(0, HD)], weight_sem.at[0, c]
            ),
            pltpu.make_async_copy(
                wv_hbm.at[0, band], wkv.at[band, pl.ds(HD, HD)], weight_sem.at[1, c]
            ),
        ]

    def query_weights(c):
        band = pl.ds(c * chunk, chunk)
        return pltpu.make_async_copy(wq_hbm.at[0, band], wq.at[band], weight_sem.at[2, c])

    output_weights = pltpu.make_async_copy(wo_hbm.at[0], wo, weight_sem.at[3, 0])
    for c in range(chunks):
        for copy in shared_weights(c):
            copy.start()
        query_weights(c).start()
    output_weights.start()

    barrier = pltpu.get_barrier_semaphore()

    def greet(to_section, to_lane):
        pl.semaphore_signal(barrier, inc=1, device_id=(to_section, to_lane), device_id_type=MESH)

    for step in range(1, lanes):
        greet(section, (lane + step) % lanes)

    @pl.when(section > 0)
    def _():
        for z in range(columns):
            greet(section - 1, z * PAIR + side)

    @pl.when(section < sections - 1)
    def _():
        for z in range(columns):
            greet(section + 1, z * PAIR + side)

    neighbours = jnp.minimum(section, 1) + jnp.minimum(sections - 1 - section, 1)
    pl.semaphore_wait(barrier, lanes - 1 + columns * neighbours)

    def rows_copy(source, unit, c, step, to_section):
        to_column = (column + step) % columns
        return pltpu.make_async_remote_copy(
            src_ref=source,
            dst_ref=gathered.at[unit, c, side, column],
            send_sem=rows_send.at[unit, c, step],
            recv_sem=rows_recv.at[unit, c, column],
            device_id=(to_section, to_column * PAIR + side),
            device_id_type=MESH,
        )

    def relay_copy(unit, c, which):
        return pltpu.make_async_remote_copy(
            src_ref=gathered.at[unit, c, which],
            dst_ref=gathered.at[unit, c, which],
            send_sem=relay_send.at[unit, c],
            recv_sem=relay_recv.at[unit, c],
            device_id=(section, partner),
            device_id_type=MESH,
        )

    def kv_copy(unit, step, landing):
        to_lane = (lane + step) % lanes
        return pltpu.make_async_remote_copy(
            src_ref=kv_send.at[unit, to_lane],
            dst_ref=kv_land.at[unit, landing],
            send_sem=kv_send_sem.at[unit, step],
            recv_sem=kv_recv_sem.at[unit, step],
            device_id=(section, to_lane),
            device_id_type=MESH,
        )

    def pair_copy(unit, c):
        return pltpu.make_async_remote_copy(
            src_ref=partial.at[unit, c, other],
            dst_ref=pair_land.at[unit, c],
            send_sem=pair_send.at[unit, c],
            recv_sem=pair_recv.at[unit, c],
            device_id=(section, partner),
            device_id_type=MESH,
        )

    def column_copy(unit, c, step):
        to_column = (column + step) % columns
        return pltpu.make_async_remote_copy(
            src_ref=column_sum.at[unit, c, to_column],
            dst_ref=column_land.at[unit, c, step],
            send_sem=column_send.at[unit, c, step],
            recv_sem=column_recv.at[unit, c, step],
            device_id=(section, to_column * PAIR + side),
            device_id_type=MESH,
        )

    def trade_copy(step, landing):
        to_lane = (lane + step) % lanes
        return pltpu.make_async_remote_copy(
            src_ref=trade_send.at[to_lane],
            dst_ref=trade_land.at[:, landing],
            send_sem=trade_send_sem.at[step],
            recv_sem=trade_recv_sem.at[step],
            device_id=(section, to_lane),
            device_id_type=MESH,
        )

    def token_rows(unit, c):
        return tokens.at[unit // block_count, unit % block_count, :, pl.ds(c * chunk, chunk)]

    @pl.when(section == 0)
    def _():
        @pl.loop(0, units)
        def _(unit):
            for c in range(chunks):
                for step in range(1, columns):
                    rows_copy(token_rows(unit, c), unit, c, step, section).start()
                pltpu.make_async_copy(
                    token_rows(unit, c),
                    gathered.at[unit, c, side, column],
                    own_sem.at[unit, c],
                ).start()

    key_cache[...] = jnp.zeros_like(key_cache)
    value_cache[...] = jnp.zeros_like(value_cache)

    trades = section == TRADER
    mixer[...] = regroup[...]

    @pl.when(trades)
    def _():
        for c in range(chunks):
            for copy in shared_weights(c):
                copy.wait()

        @pl.loop(0, width // PIECE)
        def _(part):
            band = pl.ds(pl.multiple_of(part * PIECE, PIECE), PIECE)
            for i in range(2):
                turned = lax.dot_general(
                    regroup[...],
                    wkv[band, pl.ds(i * HD, HD)],
                    (((1,), (1,)), ((), ())),
                    preferred_element_type=jnp.float32,
                ).astype(jnp.bfloat16)
                trade_send[:, i, :, band] = turned.reshape(lanes, HD // lanes, PIECE)

        for step in range(1, lanes):
            trade_copy(step, lane).start()
        trade_land[:, lane] = trade_send[lane]
        for step in range(1, lanes):
            trade_copy(step, (lane + lanes - step) % lanes).wait_recv()

        line = lax.broadcasted_iota(jnp.int32, (HD, HD), 0)
        entry = lax.broadcasted_iota(jnp.int32, (HD, HD), 1)
        mixer[...] = jnp.where(line == entry, 1.0, 0.0).astype(jnp.bfloat16)

        @pl.loop(0, width // PIECE)
        def _(part):
            band = pl.ds(pl.multiple_of(part * PIECE, PIECE), PIECE)
            for i in range(2):
                wkv[band, pl.ds(i * HD, HD)] = lax.dot_general(
                    trade_land[i, :, :, band].reshape(HD, PIECE),
                    mixer[...],
                    (((0,), (0,)), ((), ())),
                    preferred_element_type=jnp.float32,
                ).astype(jnp.bfloat16)

        for step in range(1, lanes):
            trade_copy(step, lane).wait_send()

    def receive(unit, c):
        for step in range(1, columns):
            from_column = (column + step) % columns
            pltpu.make_async_remote_copy(
                src_ref=gathered.at[unit, c, side, from_column],
                dst_ref=gathered.at[unit, c, side, from_column],
                send_sem=rows_send.at[unit, c, step],
                recv_sem=rows_recv.at[unit, c, from_column],
                device_id=(section, partner),
                device_id_type=MESH,
            ).wait_recv()

        @pl.when(section == 0)
        def _():
            pltpu.make_async_copy(
                token_rows(unit, c),
                gathered.at[unit, c, side, column],
                own_sem.at[unit, c],
            ).wait()

        @pl.when(section > 0)
        def _():
            rows_copy(finished.at[unit, c], unit, c, 0, section - 1).wait_recv()

        relay_copy(unit, c, side).start()

    def absorb(unit, c):
        relay_copy(unit, c, other).wait_recv()
        cols = pl.ds(c * chunk, chunk)
        gain = gain_row[:, cols].astype(jnp.float32)
        for z in range(columns):
            band = slice(z * PAIR * rows, (z + 1) * PAIR * rows)
            x = jnp.concatenate(
                [gathered[unit, c, i, z].astype(jnp.float32) for i in range(PAIR)], axis=0
            )
            square = jnp.sum(x * x, axis=-1, keepdims=True)
            if c == 0:
                squares[band, :] = jnp.broadcast_to(square, (PAIR * rows, HD))
            else:
                squares[band, :] += square
            normed[band, :] = (x * gain).astype(jnp.bfloat16)
        product = jnp.dot(normed[...], wkv[cols, :], preferred_element_type=jnp.float32)
        if c == 0:
            projected[:, pl.ds(query_cols, 2 * HD)] = product
        else:
            projected[:, pl.ds(query_cols, 2 * HD)] += product

    def absorb_queries(c):
        @pl.loop(0, query_cols // SPAN)
        def _(part):
            place = pl.ds(pl.multiple_of(part * SPAN, SPAN), SPAN)
            product = jnp.dot(
                normed[...],
                wq[pl.ds(c * chunk, chunk), place],
                preferred_element_type=jnp.float32,
            )
            if c == 0:
                projected[:, place] = product
            else:
                projected[:, place] += product

    def row_factor():
        return lax.rsqrt(squares[:, :1] * (1.0 / width) + EPSILON)

    def share_keys(unit):
        key_value = projected[:, pl.ds(query_cols, 2 * HD)] * row_factor()
        stacked = jnp.concatenate([key_value[:, :HD], key_value[:, HD:]], axis=0)
        turned = lax.dot_general(
            mixer[...],
            stacked.astype(jnp.bfloat16),
            (((1,), (1,)), ((), ())),
            preferred_element_type=jnp.float32,
        ).astype(jnp.bfloat16)
        turned = turned.reshape(lanes, HD // lanes, 2 * block_len)

        @pl.when(trades)
        def _():
            kv_land[unit] = turned

        @pl.when(section != TRADER)
        def _():
            kv_send[unit] = turned
            for step in range(1, lanes):
                kv_copy(unit, step, lane).start()
            kv_land[unit, lane] = kv_send[unit, lane]

    def attend(unit):
        micro = unit // block_count
        block = unit % block_count
        factor = row_factor()
        cosine = cos_rows[block]
        sine = sin_rows[block]
        for h in range(heads):
            head = projected[:, pl.ds(h * HD, HD)] * factor
            turned_head = head * cosine + pltpu.roll(head, HD // 2, 1) * sine
            queries[pl.ds(h * block_len, block_len), :] = turned_head.astype(jnp.bfloat16)

        @pl.when(section != TRADER)
        def _():
            for step in range(1, lanes):
                kv_copy(unit, step, (lane + lanes - step) % lanes).wait_recv()

        landed = kv_land[unit].reshape(HD, 2 * block_len).astype(jnp.float32)
        lower = landed[: HD // 2]
        upper = landed[HD // 2 :]
        cosine_col = cos_cols[block]
        sine_col = sin_cols[block]
        rotated = jnp.concatenate(
            [lower * cosine_col - upper * sine_col, upper * cosine_col + lower * sine_col], axis=0
        )
        place = lax.broadcasted_iota(jnp.int32, (HD, seq_len), 1)
        fresh = place // block_len == block
        swapped = jnp.where(block == 0, rotated, pltpu.roll(rotated, block_len, 1))
        keys = jnp.where(fresh, swapped, key_cache[micro].astype(jnp.float32)).astype(jnp.bfloat16)
        key_cache[micro] = keys
        swapped = jnp.where(block == 0, pltpu.roll(landed, block_len, 1), landed)
        values = jnp.where(fresh, swapped, value_cache[micro].astype(jnp.float32)).astype(
            jnp.bfloat16
        )
        value_cache[micro] = values

        stack = heads * block_len
        position = (
            lax.broadcasted_iota(jnp.int32, (stack, seq_len), 0) % block_len + block * block_len
        )
        key_position = lax.broadcasted_iota(jnp.int32, (stack, seq_len), 1)
        scores = jnp.dot(queries[...], keys, preferred_element_type=jnp.float32) * score_scale
        piece = jnp.where(key_position <= position, jnp.exp(scores), 0.0)
        denominator = jnp.sum(piece, axis=-1, keepdims=True)
        result = lax.dot_general(
            (piece / denominator).astype(jnp.bfloat16),
            values,
            (((1,), (1,)), ((), ())),
            preferred_element_type=jnp.float32,
        ).astype(jnp.bfloat16)
        for h in range(heads):
            context[:, pl.ds(h * HD, HD)] = result[h * block_len : (h + 1) * block_len]

    def down(unit, c):
        tile = TILE

        @pl.loop(0, chunk // tile)
        def _(n):
            start = pl.multiple_of(n * tile, tile)
            product = jnp.dot(
                context[...],
                wo[:, pl.ds(pl.multiple_of(c * chunk + start, tile), tile)],
                preferred_element_type=jnp.float32,
            )
            blocks = product.reshape(columns, PAIR, rows, tile).astype(jnp.bfloat16)
            for i in range(PAIR):
                partial[unit, c, i, :, :, pl.ds(start, tile)] = blocks[:, i]

        pair_copy(unit, c).start()

    def add_pair(unit, c):
        pair_copy(unit, c).wait_recv()
        for z in range(columns):
            column_sum[unit, c, z] = (
                partial[unit, c, side, z].astype(jnp.float32)
                + pair_land[unit, c, z].astype(jnp.float32)
            ).astype(jnp.bfloat16)
        for step in range(1, columns):
            column_copy(unit, c, step).start()

    def finish(unit, c):
        total = gathered[unit, c, side, column].astype(jnp.float32)
        total = total + column_sum[unit, c, column].astype(jnp.float32)
        for step in range(1, columns):
            column_copy(unit, c, step).wait_recv()
            total = total + column_land[unit, c, step].astype(jnp.float32)
        result = total.astype(jnp.bfloat16)
        finished[unit, c] = result
        out[0, unit // block_count, unit % block_count, :, pl.ds(c * chunk, chunk)] = result

        @pl.when(section < sections - 1)
        def _():
            for step in range(columns):
                rows_copy(finished.at[unit, c], unit, c, step, section + 1).start()

    @pl.when(section == 0)
    def _():
        for c in range(chunks):
            receive(0, c)

    @pl.loop(0, units + 1)
    def _(turn):
        older = turn - 1

        def step_of(name, c):
            if name == "D":
                down(older, c)
            elif name == "P":
                add_pair(older, c)
            elif name == "F":
                finish(older, c)
            elif name == "R":
                @pl.when(section > 0)
                def _():
                    receive(turn, c)
            elif name == "E":
                @pl.when((section == 0) & (turn < units - 1))
                def _():
                    receive(turn + 1, c)
            elif name == "A":

                @pl.when(turn == 0)
                def _():
                    query_weights(c).wait()

                @pl.when((turn == 0) & (section != TRADER))
                def _():
                    for copy in shared_weights(c):
                        copy.wait()

                absorb(turn, c)
                if c < chunks - 1:
                    absorb_queries(c)
            elif name == "K":
                share_keys(turn)
                absorb_queries(chunks - 1)
            elif name == "T":
                attend(turn)

                @pl.when(turn == 0)
                def _():
                    output_weights.wait()

        groups = []
        for word in SCHEDULE:
            late = word[0] in "DPF"
            if not groups or groups[-1][0] != late:
                groups.append((late, []))
            groups[-1][1].append((word[0], int(word[1:] or 0)))
        for late, members in groups:
            @pl.when((turn > 0) if late else (turn < units))
            def _():
                for name, c in members:
                    step_of(name, c)

    @pl.loop(0, units)
    def _(unit):
        for c in range(chunks):
            relay_copy(unit, c, side).wait_send()
            pair_copy(unit, c).wait_send()
            for step in range(1, columns):
                column_copy(unit, c, step).wait_send()

        @pl.when(section != TRADER)
        def _():
            for step in range(1, lanes):
                kv_copy(unit, step, lane).wait_send()

    @pl.when(section == 0)
    def _():
        @pl.loop(0, units)
        def _(unit):
            for c in range(chunks):
                for step in range(1, columns):
                    rows_copy(token_rows(unit, c), unit, c, step, section).wait_send()

    @pl.when(section < sections - 1)
    def _():
        @pl.loop(0, units)
        def _(unit):
            for c in range(chunks):
                for step in range(columns):
                    rows_copy(finished.at[unit, c], unit, c, step, section + 1).wait_send()


def kernel_body(tokens, norm_gain, w_query, w_key, w_value, w_out):
    sections = lax.axis_size("section")
    lanes = lax.axis_size("tensor")
    micro_count, block_count, rows, width = tokens.shape
    query_cols = w_query.shape[2]
    block_len = rows * lanes
    seq_len = block_count * block_len
    units = micro_count * block_count
    columns = lanes // PAIR
    chunks = CHUNKS
    chunk = width // chunks
    half = HD // 2
    frequency = np.power(
        np.float32(ROPE_BASE), -(np.arange(half, dtype=np.float32) * np.float32(2.0)) / np.float32(HD)
    )
    angles = np.arange(seq_len, dtype=np.float32)[:, None] * frequency[None, :]
    cosine, sine = np.cos(angles), np.sin(angles)
    cos_rows = np.concatenate([cosine, cosine], axis=1).reshape(block_count, block_len, HD)
    sin_rows = np.concatenate([-sine, sine], axis=1).reshape(block_count, block_len, HD)

    def by_column(table):
        table = np.swapaxes(table.reshape(block_count, block_len, half), 1, 2)
        return np.concatenate([table, table], axis=2)

    entries = HD // KV_HEADS
    target = np.arange(HD)
    source = (target % entries) * KV_HEADS + target // entries
    regroup = (source[:, None] == np.arange(HD)[None, :]).astype(jnp.bfloat16)
    dims = (sections, lanes, micro_count, block_count, rows, width, chunks, query_cols)
    vmem = pl.BlockSpec(memory_space=pltpu.VMEM)
    hbm = pl.BlockSpec(memory_space=pl.ANY)
    dma = pltpu.SemaphoreType.DMA
    bf16 = jnp.bfloat16
    return pl.pallas_call(
        functools.partial(layer_kernel, dims),
        out_shape=jax.ShapeDtypeStruct((1,) + tokens.shape, bf16),
        in_specs=[vmem] * 7 + [hbm] * 4,
        out_specs=vmem,
        scratch_shapes=[
            pltpu.VMEM((width, query_cols), bf16),
            pltpu.VMEM((width, 2 * HD), bf16),
            pltpu.VMEM((query_cols, width), bf16),
            pltpu.VMEM((units, chunks, PAIR, columns, rows, chunk), bf16),
            pltpu.VMEM((block_len, chunk), bf16),
            pltpu.VMEM((block_len, HD), jnp.float32),
            pltpu.VMEM((block_len, query_cols + 2 * HD), jnp.float32),
            pltpu.VMEM((query_cols // HD * block_len, HD), bf16),
            pltpu.VMEM((block_len, query_cols), bf16),
            pltpu.VMEM((units, lanes, HD // lanes, 2 * block_len), bf16),
            pltpu.VMEM((units, lanes, HD // lanes, 2 * block_len), bf16),
            pltpu.VMEM((micro_count, HD, seq_len), bf16),
            pltpu.VMEM((micro_count, HD, seq_len), bf16),
            pltpu.VMEM((units, chunks, PAIR, columns, rows, chunk), bf16),
            pltpu.VMEM((units, chunks, columns, rows, chunk), bf16),
            pltpu.VMEM((units, chunks, columns, rows, chunk), bf16),
            pltpu.VMEM((units, chunks, columns, rows, chunk), bf16),
            pltpu.VMEM((units, chunks, rows, chunk), bf16),
            dma((4, chunks)),
            dma((units, chunks)),
            dma((units, chunks, columns)),
            dma((units, chunks, columns)),
            dma((units, chunks)),
            dma((units, chunks)),
            dma((units, lanes)),
            dma((units, lanes)),
            dma((units, chunks)),
            dma((units, chunks)),
            dma((units, chunks, columns)),
            dma((units, chunks, columns)),
            pltpu.VMEM((HD, HD), bf16),
            pltpu.VMEM((lanes, 2, HD // lanes, width), bf16),
            pltpu.VMEM((2, lanes, HD // lanes, width), bf16),
            dma((lanes,)),
            dma((lanes,)),
        ],
        compiler_params=pltpu.CompilerParams(
            collective_id=0, has_side_effects=True, vmem_limit_bytes=67043328
        ),
    )(
        tokens,
        norm_gain,
        jnp.asarray(cos_rows),
        jnp.asarray(sin_rows),
        jnp.asarray(by_column(cosine)),
        jnp.asarray(by_column(sine)),
        jnp.asarray(regroup),
        w_query,
        w_key,
        w_value,
        w_out,
    )


CHUNKS = 4
SPAN = 1024
TILE = 2048
TRADER = 2
PIECE = 1024
SCHEDULE = ("D0", "D1", "D2", "D3", "P0", "P1", "E0", "E1", "R0", "P2", "R1", "P3", "R2", "E2", "E3", "F0", "R3", "A0", "F1", "A1", "F2", "A2", "F3", "A3", "K", "T")


def body(tokens, norm_gain, w_query, w_key, w_value, w_out):
    lanes = lax.axis_size("tensor")
    fits = (
        lanes == KV_HEADS
        and w_key.shape[2] == HD
        and w_query.shape[2] == HEADS // KV_HEADS * HD
        and tokens.shape[2] == 8
        and tokens.shape[2] * lanes * 2 == HD
        and tokens.shape[1] == 2
        and tokens.shape[3] % (CHUNKS * TILE) == 0
        and w_query.shape[2] % SPAN == 0
        and tokens.shape[3] % PIECE == 0
    )
    chosen = kernel_body if fits else general_body
    return chosen(tokens, norm_gain, w_query, w_key, w_value, w_out)


def solution(mesh):
    return jax.shard_map(
        body,
        mesh=mesh,
        in_specs=(
            P(None, None, "tensor", None),
            P("section", None),
            P("section", None, "tensor"),
            P("section", None, "tensor"),
            P("section", None, "tensor"),
            P("section", "tensor", None),
        ),
        out_specs=P("section", None, None, "tensor", None),
        check_vma=False,
    )
```

```python
import functools
import math

import jax
import jax.numpy as jnp
import numpy as np
from jax import lax
from jax.experimental import pallas as pl
from jax.experimental.pallas import tpu as pltpu
from jax.sharding import PartitionSpec as P

HEADS = 64
KV_HEADS = 8
HD = 128


EPSILON = 1e-05
ROPE_BASE = 500000.0


def shifted(block, axis, distance):
    devices = range(lax.axis_size(axis))
    route = [(i - distance, i) for i in devices if i - distance in devices]
    return lax.ppermute(block, axis, route)


def rotate(field, positions):
    half_dim = field.shape[-1] // 2
    frequency = ROPE_BASE ** (-(jnp.arange(half_dim, dtype=jnp.float32) * 2.0) / field.shape[-1])
    angles = positions.astype(jnp.float32)[:, None] * frequency[None, :]
    cosine_table = jnp.cos(angles)[:, None, :]
    sine_table = jnp.sin(angles)[:, None, :]
    lower_half = field[..., :half_dim]
    upper_half = field[..., half_dim:]
    return jnp.concatenate(
        [
            lower_half * cosine_table - upper_half * sine_table,
            upper_half * cosine_table + lower_half * sine_table,
        ],
        axis=-1,
    )


def normalize(activations, gain_row):
    widened = activations.astype(jnp.float32)
    factor = lax.rsqrt(jnp.mean(widened * widened, axis=-1, keepdims=True) + EPSILON)
    return (widened * factor * gain_row.astype(jnp.float32)).astype(jnp.bfloat16)


def general_body(tokens, norm_gain, w_query, w_key, w_value, w_out):
    section_count = lax.axis_size("section")
    section_index = lax.axis_index("section")
    lane_count = lax.axis_size("tensor")
    lane_index = lax.axis_index("tensor")
    micro_count, block_count, shard_rows, model_width = tokens.shape
    block_len = shard_rows * lane_count
    seq_len = block_count * block_len
    unit_count = micro_count * block_count
    tick_count = unit_count + section_count - 1
    gain_row = norm_gain[0]
    w_joined = jnp.concatenate([w_query[0], w_key[0], w_value[0]], axis=1)
    w_down = w_out[0]
    query_cols = w_query.shape[2]
    key_cols = w_key.shape[2]
    local_heads = query_cols // HD
    kv_index = lane_index * local_heads // (HEADS // KV_HEADS)
    score_scale = 1.0 / math.sqrt(HD)
    offsets = jnp.arange(block_len, dtype=jnp.int32)
    key_positions = jnp.arange(seq_len, dtype=jnp.int32)
    incoming = jnp.zeros((shard_rows, model_width), jnp.bfloat16)
    key_cache = jnp.zeros((micro_count, seq_len, HD), jnp.bfloat16)
    value_cache = jnp.zeros((micro_count, seq_len, HD), jnp.bfloat16)
    stored = jnp.zeros((micro_count, block_count, shard_rows, model_width), jnp.bfloat16)

    def attend(projected, batch_index, block_index, key_cache, value_cache):
        queries = projected[:, :query_cols].reshape(block_len, local_heads, HD)
        key_value = projected[:, query_cols:].astype(jnp.bfloat16)
        gathered = lax.all_gather(key_value, "tensor", axis=1, tiled=True)
        gathered = gathered.reshape(block_len, lane_count, 2, key_cols)
        keys_all = gathered[:, :, 0, :].reshape(block_len, HD, KV_HEADS)
        values_all = gathered[:, :, 1, :].reshape(block_len, HD, KV_HEADS)
        key_new = lax.dynamic_index_in_dim(keys_all, kv_index, 2, keepdims=False)
        value_new = lax.dynamic_index_in_dim(values_all, kv_index, 2, keepdims=False)
        positions = block_index * block_len + offsets
        queries = rotate(queries, positions).astype(jnp.bfloat16)
        key_new = rotate(key_new.astype(jnp.float32)[:, None, :], positions)[:, 0, :].astype(
            jnp.bfloat16
        )
        key_cache = lax.dynamic_update_slice(
            key_cache, key_new[None], (batch_index, block_index * block_len, 0)
        )
        value_cache = lax.dynamic_update_slice(
            value_cache, value_new[None], (batch_index, block_index * block_len, 0)
        )
        key_rows = lax.dynamic_index_in_dim(key_cache, batch_index, 0, keepdims=False)
        value_rows = lax.dynamic_index_in_dim(value_cache, batch_index, 0, keepdims=False)
        scores = (
            jnp.einsum("qhd,kd->hqk", queries, key_rows, preferred_element_type=jnp.float32)
            * score_scale
        )
        visible = key_positions[None, :] <= positions[:, None]
        weights = jnp.where(visible[None], jnp.exp(scores), 0.0)
        weights = (weights / jnp.sum(weights, axis=-1, keepdims=True)).astype(jnp.bfloat16)
        context = jnp.einsum("hqk,kd->qhd", weights, value_rows, preferred_element_type=jnp.float32)
        context = context.astype(jnp.bfloat16).reshape(block_len, query_cols)
        reduced = lax.psum_scatter(
            jnp.dot(context, w_down, preferred_element_type=jnp.float32).astype(jnp.bfloat16),
            "tensor",
            scatter_dimension=0,
            tiled=True,
        ).astype(jnp.float32)
        return (reduced, key_cache, value_cache)

    def advance(tick_index, state_tuple):
        incoming, key_cache, value_cache, stored = state_tuple
        unit_index = tick_index - section_index
        usable = (unit_index >= 0) & (unit_index < unit_count)
        unit_index = jnp.clip(unit_index, 0, unit_count - 1)
        batch_index = unit_index // block_count
        block_index = unit_index % block_count
        arriving = lax.dynamic_slice(
            tokens, (batch_index, block_index, 0, 0), (1, 1, incoming.shape[0], model_width)
        )[0, 0]
        present = jnp.where(section_index == 0, arriving, incoming)
        projected = jnp.dot(
            lax.all_gather(normalize(present, gain_row), "tensor", axis=0, tiled=True),
            w_joined,
            preferred_element_type=jnp.float32,
        )
        reduced, key_cache, value_cache = attend(
            projected, batch_index, block_index, key_cache, value_cache
        )
        result = (present.astype(jnp.float32) + reduced).astype(jnp.bfloat16)
        previous = lax.dynamic_slice(
            stored, (batch_index, block_index, 0, 0), (1, 1, shard_rows, model_width)
        )[0, 0]
        chosen = jnp.where(usable, result, previous)
        stored = lax.dynamic_update_slice(
            stored, chosen[None, None], (batch_index, block_index, 0, 0)
        )
        incoming = shifted(result, "section", 1)
        return (incoming, key_cache, value_cache, stored)

    final_state = lax.fori_loop(0, tick_count, advance, (incoming, key_cache, value_cache, stored))
    return final_state[3][None]


PAIR = 2
MESH = pl.DeviceIdType.MESH


def layer_kernel(
    dims,
    tokens,
    gain_row,
    cos_rows,
    sin_rows,
    cos_cols,
    sin_cols,
    regroup,
    wq_hbm,
    wk_hbm,
    wv_hbm,
    wo_hbm,
    out,
    wq,
    wkv,
    wo,
    gathered,
    normed,
    squares,
    projected,
    queries,
    context,
    kv_send,
    kv_land,
    key_cache,
    value_cache,
    partial,
    pair_land,
    column_sum,
    column_land,
    finished,
    weight_sem,
    own_sem,
    rows_send,
    rows_recv,
    relay_send,
    relay_recv,
    kv_send_sem,
    kv_recv_sem,
    pair_send,
    pair_recv,
    column_send,
    column_recv,
    mixer,
    trade_send,
    trade_land,
    trade_send_sem,
    trade_recv_sem,
):
    sections, lanes, micro_count, block_count, rows, width, chunks, query_cols = dims
    columns = lanes // PAIR
    units = micro_count * block_count
    chunk = width // chunks
    block_len = rows * lanes
    seq_len = block_count * block_len
    heads = query_cols // HD
    section = lax.axis_index("section")
    lane = lax.axis_index("tensor")
    column = lane // PAIR
    side = lane % PAIR
    other = 1 - side
    partner = column * PAIR + other
    score_scale = 1.0 / math.sqrt(HD)

    def shared_weights(c):
        band = pl.ds(c * chunk, chunk)
        return [
            pltpu.make_async_copy(
                wk_hbm.at[0, band], wkv.at[band, pl.ds(0, HD)], weight_sem.at[0, c]
            ),
            pltpu.make_async_copy(
                wv_hbm.at[0, band], wkv.at[band, pl.ds(HD, HD)], weight_sem.at[1, c]
            ),
        ]

    def query_weights(c):
        band = pl.ds(c * chunk, chunk)
        return pltpu.make_async_copy(wq_hbm.at[0, band], wq.at[band], weight_sem.at[2, c])

    output_weights = pltpu.make_async_copy(wo_hbm.at[0], wo, weight_sem.at[3, 0])
    for c in range(chunks):
        for copy in shared_weights(c):
            copy.start()
        query_weights(c).start()
    output_weights.start()

    barrier = pltpu.get_barrier_semaphore()

    def greet(to_section, to_lane):
        pl.semaphore_signal(barrier, inc=1, device_id=(to_section, to_lane), device_id_type=MESH)

    for step in range(1, lanes):
        greet(section, (lane + step) % lanes)

    @pl.when(section > 0)
    def _():
        for z in range(columns):
            greet(section - 1, z * PAIR + side)

    @pl.when(section < sections - 1)
    def _():
        for z in range(columns):
            greet(section + 1, z * PAIR + side)

    neighbours = jnp.minimum(section, 1) + jnp.minimum(sections - 1 - section, 1)
    pl.semaphore_wait(barrier, lanes - 1 + columns * neighbours)

    def opposite(step):
        if step == 0:
            return column
        if step == 1:
            return column + 1 - 2 * (column % 2)
        if step == 2:
            return (column + 2) % columns
        return columns - 1 - column

    def rows_copy(source, unit, c, step, to_section):
        to_column = opposite(step)
        return pltpu.make_async_remote_copy(
            src_ref=source,
            dst_ref=gathered.at[unit, c, side, column],
            send_sem=rows_send.at[unit, c, step],
            recv_sem=rows_recv.at[unit, c, column],
            device_id=(to_section, to_column * PAIR + side),
            device_id_type=MESH,
        )

    def relay_copy(unit, c, which):
        return pltpu.make_async_remote_copy(
            src_ref=gathered.at[unit, c, which],
            dst_ref=gathered.at[unit, c, which],
            send_sem=relay_send.at[unit, c],
            recv_sem=relay_recv.at[unit, c],
            device_id=(section, partner),
            device_id_type=MESH,
        )

    def kv_copy(unit, step, landing):
        to_lane = (lane + step) % lanes
        return pltpu.make_async_remote_copy(
            src_ref=kv_send.at[unit, to_lane],
            dst_ref=kv_land.at[unit, landing],
            send_sem=kv_send_sem.at[unit, step],
            recv_sem=kv_recv_sem.at[unit, step],
            device_id=(section, to_lane),
            device_id_type=MESH,
        )

    def pair_copy(unit, c):
        return pltpu.make_async_remote_copy(
            src_ref=partial.at[unit, c, other],
            dst_ref=pair_land.at[unit, c],
            send_sem=pair_send.at[unit, c],
            recv_sem=pair_recv.at[unit, c],
            device_id=(section, partner),
            device_id_type=MESH,
        )

    def column_copy(unit, c, step):
        to_column = opposite(step)
        return pltpu.make_async_remote_copy(
            src_ref=column_sum.at[unit, c, to_column],
            dst_ref=column_land.at[unit, c, step],
            send_sem=column_send.at[unit, c, step],
            recv_sem=column_recv.at[unit, c, step],
            device_id=(section, to_column * PAIR + side),
            device_id_type=MESH,
        )

    def trade_copy(step, landing):
        to_lane = (lane + step) % lanes
        return pltpu.make_async_remote_copy(
            src_ref=trade_send.at[to_lane],
            dst_ref=trade_land.at[:, landing],
            send_sem=trade_send_sem.at[step],
            recv_sem=trade_recv_sem.at[step],
            device_id=(section, to_lane),
            device_id_type=MESH,
        )

    def token_rows(unit, c):
        return tokens.at[unit // block_count, unit % block_count, :, pl.ds(c * chunk, chunk)]

    @pl.when(section == 0)
    def _():
        @pl.loop(0, units)
        def _(unit):
            for c in range(chunks):
                for step in range(1, columns):
                    rows_copy(token_rows(unit, c), unit, c, step, section).start()
                pltpu.make_async_copy(
                    token_rows(unit, c),
                    gathered.at[unit, c, side, column],
                    own_sem.at[unit, c],
                ).start()

    key_cache[...] = jnp.zeros_like(key_cache)
    value_cache[...] = jnp.zeros_like(value_cache)

    trades = section == TRADER
    mixer[...] = regroup[...]

    @pl.when(trades)
    def _():
        for c in range(chunks):
            for copy in shared_weights(c):
                copy.wait()

        @pl.loop(0, width // PIECE)
        def _(part):
            band = pl.ds(pl.multiple_of(part * PIECE, PIECE), PIECE)
            for i in range(2):
                turned = lax.dot_general(
                    regroup[...],
                    wkv[band, pl.ds(i * HD, HD)],
                    (((1,), (1,)), ((), ())),
                    preferred_element_type=jnp.float32,
                ).astype(jnp.bfloat16)
                trade_send[:, i, :, band] = turned.reshape(lanes, HD // lanes, PIECE)

        for step in range(1, lanes):
            trade_copy(step, lane).start()
        trade_land[:, lane] = trade_send[lane]
        for step in range(1, lanes):
            trade_copy(step, (lane + lanes - step) % lanes).wait_recv()

        line = lax.broadcasted_iota(jnp.int32, (HD, HD), 0)
        entry = lax.broadcasted_iota(jnp.int32, (HD, HD), 1)
        mixer[...] = jnp.where(line == entry, 1.0, 0.0).astype(jnp.bfloat16)

        @pl.loop(0, width // PIECE)
        def _(part):
            band = pl.ds(pl.multiple_of(part * PIECE, PIECE), PIECE)
            for i in range(2):
                wkv[band, pl.ds(i * HD, HD)] = lax.dot_general(
                    trade_land[i, :, :, band].reshape(HD, PIECE),
                    mixer[...],
                    (((0,), (0,)), ((), ())),
                    preferred_element_type=jnp.float32,
                ).astype(jnp.bfloat16)

        for step in range(1, lanes):
            trade_copy(step, lane).wait_send()

    def receive(unit, c):
        for step in range(1, columns):
            from_column = (column + step) % columns
            pltpu.make_async_remote_copy(
                src_ref=gathered.at[unit, c, side, from_column],
                dst_ref=gathered.at[unit, c, side, from_column],
                send_sem=rows_send.at[unit, c, step],
                recv_sem=rows_recv.at[unit, c, from_column],
                device_id=(section, partner),
                device_id_type=MESH,
            ).wait_recv()

        @pl.when(section == 0)
        def _():
            pltpu.make_async_copy(
                token_rows(unit, c),
                gathered.at[unit, c, side, column],
                own_sem.at[unit, c],
            ).wait()

        @pl.when(section > 0)
        def _():
            rows_copy(finished.at[unit, c], unit, c, 0, section - 1).wait_recv()

        relay_copy(unit, c, side).start()

    def absorb(unit, c):
        relay_copy(unit, c, other).wait_recv()
        cols = pl.ds(c * chunk, chunk)
        gain = gain_row[:, cols].astype(jnp.float32)
        for z in range(columns):
            band = slice(z * PAIR * rows, (z + 1) * PAIR * rows)
            x = jnp.concatenate(
                [gathered[unit, c, i, z].astype(jnp.float32) for i in range(PAIR)], axis=0
            )
            square = jnp.sum(x * x, axis=-1, keepdims=True)
            if c == 0:
                squares[band, :] = jnp.broadcast_to(square, (PAIR * rows, HD))
            else:
                squares[band, :] += square
            normed[band, :] = (x * gain).astype(jnp.bfloat16)
        product = jnp.dot(normed[...], wkv[cols, :], preferred_element_type=jnp.float32)
        if c == 0:
            projected[:, pl.ds(query_cols, 2 * HD)] = product
        else:
            projected[:, pl.ds(query_cols, 2 * HD)] += product

    def absorb_queries(c):
        @pl.loop(0, query_cols // SPAN)
        def _(part):
            place = pl.ds(pl.multiple_of(part * SPAN, SPAN), SPAN)
            product = jnp.dot(
                normed[...],
                wq[pl.ds(c * chunk, chunk), place],
                preferred_element_type=jnp.float32,
            )
            if c == 0:
                projected[:, place] = product
            else:
                projected[:, place] += product

    def row_factor():
        return lax.rsqrt(squares[:, :1] * (1.0 / width) + EPSILON)

    def share_keys(unit):
        key_value = projected[:, pl.ds(query_cols, 2 * HD)] * row_factor()
        stacked = jnp.concatenate([key_value[:, :HD], key_value[:, HD:]], axis=0)
        turned = lax.dot_general(
            mixer[...],
            stacked.astype(jnp.bfloat16),
            (((1,), (1,)), ((), ())),
            preferred_element_type=jnp.float32,
        ).astype(jnp.bfloat16)
        turned = turned.reshape(lanes, HD // lanes, 2 * block_len)

        @pl.when(trades)
        def _():
            kv_land[unit] = turned

        @pl.when(section != TRADER)
        def _():
            kv_send[unit] = turned
            for step in range(1, lanes):
                kv_copy(unit, step, lane).start()
            kv_land[unit, lane] = kv_send[unit, lane]

    def attend(unit):
        micro = unit // block_count
        block = unit % block_count
        factor = row_factor()
        cosine = cos_rows[block]
        sine = sin_rows[block]
        for h in range(heads):
            head = projected[:, pl.ds(h * HD, HD)] * factor
            turned_head = head * cosine + pltpu.roll(head, HD // 2, 1) * sine
            queries[pl.ds(h * block_len, block_len), :] = turned_head.astype(jnp.bfloat16)

        @pl.when(section != TRADER)
        def _():
            for step in range(1, lanes):
                kv_copy(unit, step, (lane + lanes - step) % lanes).wait_recv()

        landed = kv_land[unit].reshape(HD, 2 * block_len).astype(jnp.float32)
        lower = landed[: HD // 2]
        upper = landed[HD // 2 :]
        cosine_col = cos_cols[block]
        sine_col = sin_cols[block]
        rotated = jnp.concatenate(
            [lower * cosine_col - upper * sine_col, upper * cosine_col + lower * sine_col], axis=0
        )
        place = lax.broadcasted_iota(jnp.int32, (HD, seq_len), 1)
        fresh = place // block_len == block
        swapped = jnp.where(block == 0, rotated, pltpu.roll(rotated, block_len, 1))
        keys = jnp.where(fresh, swapped, key_cache[micro].astype(jnp.float32)).astype(jnp.bfloat16)
        key_cache[micro] = keys
        swapped = jnp.where(block == 0, pltpu.roll(landed, block_len, 1), landed)
        values = jnp.where(fresh, swapped, value_cache[micro].astype(jnp.float32)).astype(
            jnp.bfloat16
        )
        value_cache[micro] = values

        stack = heads * block_len
        position = (
            lax.broadcasted_iota(jnp.int32, (stack, seq_len), 0) % block_len + block * block_len
        )
        key_position = lax.broadcasted_iota(jnp.int32, (stack, seq_len), 1)
        scores = jnp.dot(queries[...], keys, preferred_element_type=jnp.float32) * score_scale
        piece = jnp.where(key_position <= position, jnp.exp(scores), 0.0)
        denominator = jnp.sum(piece, axis=-1, keepdims=True)
        result = lax.dot_general(
            (piece / denominator).astype(jnp.bfloat16),
            values,
            (((1,), (1,)), ((), ())),
            preferred_element_type=jnp.float32,
        ).astype(jnp.bfloat16)
        for h in range(heads):
            context[:, pl.ds(h * HD, HD)] = result[h * block_len : (h + 1) * block_len]

    def down(unit, c):
        tile = TILE

        @pl.loop(0, chunk // tile)
        def _(n):
            start = pl.multiple_of(n * tile, tile)
            product = jnp.dot(
                context[...],
                wo[:, pl.ds(pl.multiple_of(c * chunk + start, tile), tile)],
                preferred_element_type=jnp.float32,
            )
            blocks = product.reshape(columns, PAIR, rows, tile).astype(jnp.bfloat16)
            for i in range(PAIR):
                partial[unit, c, i, :, :, pl.ds(start, tile)] = blocks[:, i]

        pair_copy(unit, c).start()

    def add_pair(unit, c):
        pair_copy(unit, c).wait_recv()
        for z in range(columns):
            column_sum[unit, c, z] = (
                partial[unit, c, side, z].astype(jnp.float32)
                + pair_land[unit, c, z].astype(jnp.float32)
            ).astype(jnp.bfloat16)
        for step in reversed(range(1, columns)):
            column_copy(unit, c, step).start()

    def finish(unit, c):
        total = gathered[unit, c, side, column].astype(jnp.float32)
        total = total + column_sum[unit, c, column].astype(jnp.float32)
        for step in range(1, columns):
            column_copy(unit, c, step).wait_recv()
            total = total + column_land[unit, c, step].astype(jnp.float32)
        result = total.astype(jnp.bfloat16)
        finished[unit, c] = result
        out[0, unit // block_count, unit % block_count, :, pl.ds(c * chunk, chunk)] = result

        @pl.when(section < sections - 1)
        def _():
            for step in reversed(range(columns)):
                rows_copy(finished.at[unit, c], unit, c, step, section + 1).start()

    @pl.when(section == 0)
    def _():
        for c in range(chunks):
            receive(0, c)

    @pl.loop(0, units + 1)
    def _(turn):
        older = turn - 1

        def step_of(name, c):
            if name == "D":
                down(older, c)
            elif name == "P":
                add_pair(older, c)
            elif name == "F":
                finish(older, c)
            elif name == "R":
                @pl.when(section > 0)
                def _():
                    receive(turn, c)
            elif name == "E":
                @pl.when((section == 0) & (turn < units - 1))
                def _():
                    receive(turn + 1, c)
            elif name == "A":

                @pl.when(turn == 0)
                def _():
                    query_weights(c).wait()

                @pl.when((turn == 0) & (section != TRADER))
                def _():
                    for copy in shared_weights(c):
                        copy.wait()

                absorb(turn, c)
                if c < chunks - 1:
                    absorb_queries(c)
            elif name == "K":
                share_keys(turn)
                absorb_queries(chunks - 1)
            elif name == "T":
                attend(turn)

                @pl.when(turn == 0)
                def _():
                    output_weights.wait()

        groups = []
        for word in SCHEDULE:
            late = word[0] in "DPF"
            if not groups or groups[-1][0] != late:
                groups.append((late, []))
            groups[-1][1].append((word[0], int(word[1:] or 0)))
        for late, members in groups:
            @pl.when((turn > 0) if late else (turn < units))
            def _():
                for name, c in members:
                    step_of(name, c)

    @pl.loop(0, units)
    def _(unit):
        for c in range(chunks):
            relay_copy(unit, c, side).wait_send()
            pair_copy(unit, c).wait_send()
            for step in range(1, columns):
                column_copy(unit, c, step).wait_send()

        @pl.when(section != TRADER)
        def _():
            for step in range(1, lanes):
                kv_copy(unit, step, lane).wait_send()

    @pl.when(section == 0)
    def _():
        @pl.loop(0, units)
        def _(unit):
            for c in range(chunks):
                for step in range(1, columns):
                    rows_copy(token_rows(unit, c), unit, c, step, section).wait_send()

    @pl.when(section < sections - 1)
    def _():
        @pl.loop(0, units)
        def _(unit):
            for c in range(chunks):
                for step in range(columns):
                    rows_copy(finished.at[unit, c], unit, c, step, section + 1).wait_send()


def kernel_body(tokens, norm_gain, w_query, w_key, w_value, w_out):
    sections = lax.axis_size("section")
    lanes = lax.axis_size("tensor")
    micro_count, block_count, rows, width = tokens.shape
    query_cols = w_query.shape[2]
    block_len = rows * lanes
    seq_len = block_count * block_len
    units = micro_count * block_count
    columns = lanes // PAIR
    chunks = CHUNKS
    chunk = width // chunks
    half = HD // 2
    frequency = np.power(
        np.float32(ROPE_BASE), -(np.arange(half, dtype=np.float32) * np.float32(2.0)) / np.float32(HD)
    )
    angles = np.arange(seq_len, dtype=np.float32)[:, None] * frequency[None, :]
    cosine, sine = np.cos(angles), np.sin(angles)
    cos_rows = np.concatenate([cosine, cosine], axis=1).reshape(block_count, block_len, HD)
    sin_rows = np.concatenate([-sine, sine], axis=1).reshape(block_count, block_len, HD)

    def by_column(table):
        table = np.swapaxes(table.reshape(block_count, block_len, half), 1, 2)
        return np.concatenate([table, table], axis=2)

    entries = HD // KV_HEADS
    target = np.arange(HD)
    source = (target % entries) * KV_HEADS + target // entries
    regroup = (source[:, None] == np.arange(HD)[None, :]).astype(jnp.bfloat16)
    dims = (sections, lanes, micro_count, block_count, rows, width, chunks, query_cols)
    vmem = pl.BlockSpec(memory_space=pltpu.VMEM)
    hbm = pl.BlockSpec(memory_space=pl.ANY)
    dma = pltpu.SemaphoreType.DMA
    bf16 = jnp.bfloat16
    return pl.pallas_call(
        functools.partial(layer_kernel, dims),
        out_shape=jax.ShapeDtypeStruct((1,) + tokens.shape, bf16),
        in_specs=[vmem] * 7 + [hbm] * 4,
        out_specs=vmem,
        scratch_shapes=[
            pltpu.VMEM((width, query_cols), bf16),
            pltpu.VMEM((width, 2 * HD), bf16),
            pltpu.VMEM((query_cols, width), bf16),
            pltpu.VMEM((units, chunks, PAIR, columns, rows, chunk), bf16),
            pltpu.VMEM((block_len, chunk), bf16),
            pltpu.VMEM((block_len, HD), jnp.float32),
            pltpu.VMEM((block_len, query_cols + 2 * HD), jnp.float32),
            pltpu.VMEM((query_cols // HD * block_len, HD), bf16),
            pltpu.VMEM((block_len, query_cols), bf16),
            pltpu.VMEM((units, lanes, HD // lanes, 2 * block_len), bf16),
            pltpu.VMEM((units, lanes, HD // lanes, 2 * block_len), bf16),
            pltpu.VMEM((micro_count, HD, seq_len), bf16),
            pltpu.VMEM((micro_count, HD, seq_len), bf16),
            pltpu.VMEM((units, chunks, PAIR, columns, rows, chunk), bf16),
            pltpu.VMEM((units, chunks, columns, rows, chunk), bf16),
            pltpu.VMEM((units, chunks, columns, rows, chunk), bf16),
            pltpu.VMEM((units, chunks, columns, rows, chunk), bf16),
            pltpu.VMEM((units, chunks, rows, chunk), bf16),
            dma((4, chunks)),
            dma((units, chunks)),
            dma((units, chunks, columns)),
            dma((units, chunks, columns)),
            dma((units, chunks)),
            dma((units, chunks)),
            dma((units, lanes)),
            dma((units, lanes)),
            dma((units, chunks)),
            dma((units, chunks)),
            dma((units, chunks, columns)),
            dma((units, chunks, columns)),
            pltpu.VMEM((HD, HD), bf16),
            pltpu.VMEM((lanes, 2, HD // lanes, width), bf16),
            pltpu.VMEM((2, lanes, HD // lanes, width), bf16),
            dma((lanes,)),
            dma((lanes,)),
        ],
        compiler_params=pltpu.CompilerParams(
            collective_id=0, has_side_effects=True, vmem_limit_bytes=67043328
        ),
    )(
        tokens,
        norm_gain,
        jnp.asarray(cos_rows),
        jnp.asarray(sin_rows),
        jnp.asarray(by_column(cosine)),
        jnp.asarray(by_column(sine)),
        jnp.asarray(regroup),
        w_query,
        w_key,
        w_value,
        w_out,
    )


CHUNKS = 4
SPAN = 1024
TILE = 2048
TRADER = 2
PIECE = 1024
SCHEDULE = ("D0", "D1", "D2", "D3", "P0", "P1", "E0", "E1", "R0", "P2", "R1", "P3", "R2", "E2", "E3", "F0", "R3", "A0", "F1", "A1", "F2", "A2", "F3", "A3", "K", "T")


def body(tokens, norm_gain, w_query, w_key, w_value, w_out):
    lanes = lax.axis_size("tensor")
    fits = (
        lanes == KV_HEADS
        and w_key.shape[2] == HD
        and w_query.shape[2] == HEADS // KV_HEADS * HD
        and tokens.shape[2] == 8
        and tokens.shape[2] * lanes * 2 == HD
        and tokens.shape[1] == 2
        and lanes == 4 * PAIR
        and tokens.shape[3] % (CHUNKS * TILE) == 0
        and w_query.shape[2] % SPAN == 0
        and tokens.shape[3] % PIECE == 0
    )
    chosen = kernel_body if fits else general_body
    return chosen(tokens, norm_gain, w_query, w_key, w_value, w_out)


def solution(mesh):
    return jax.shard_map(
        body,
        mesh=mesh,
        in_specs=(
            P(None, None, "tensor", None),
            P("section", None),
            P("section", None, "tensor"),
            P("section", None, "tensor"),
            P("section", None, "tensor"),
            P("section", "tensor", None),
        ),
        out_specs=P("section", None, None, "tensor", None),
        check_vma=False,
    )
```

```python
import functools
import math

import jax
import jax.numpy as jnp
import numpy as np
from jax import lax
from jax.experimental import pallas as pl
from jax.experimental.pallas import tpu as pltpu
from jax.sharding import PartitionSpec as P

HEADS = 64
KV_HEADS = 8
HD = 128


EPSILON = 1e-05
ROPE_BASE = 500000.0


def shifted(block, axis, distance):
    devices = range(lax.axis_size(axis))
    route = [(i - distance, i) for i in devices if i - distance in devices]
    return lax.ppermute(block, axis, route)


def rotate(field, positions):
    half_dim = field.shape[-1] // 2
    frequency = ROPE_BASE ** (-(jnp.arange(half_dim, dtype=jnp.float32) * 2.0) / field.shape[-1])
    angles = positions.astype(jnp.float32)[:, None] * frequency[None, :]
    cosine_table = jnp.cos(angles)[:, None, :]
    sine_table = jnp.sin(angles)[:, None, :]
    lower_half = field[..., :half_dim]
    upper_half = field[..., half_dim:]
    return jnp.concatenate(
        [
            lower_half * cosine_table - upper_half * sine_table,
            upper_half * cosine_table + lower_half * sine_table,
        ],
        axis=-1,
    )


def normalize(activations, gain_row):
    widened = activations.astype(jnp.float32)
    factor = lax.rsqrt(jnp.mean(widened * widened, axis=-1, keepdims=True) + EPSILON)
    return (widened * factor * gain_row.astype(jnp.float32)).astype(jnp.bfloat16)


def general_body(tokens, norm_gain, w_query, w_key, w_value, w_out):
    section_count = lax.axis_size("section")
    section_index = lax.axis_index("section")
    lane_count = lax.axis_size("tensor")
    lane_index = lax.axis_index("tensor")
    micro_count, block_count, shard_rows, model_width = tokens.shape
    block_len = shard_rows * lane_count
    seq_len = block_count * block_len
    unit_count = micro_count * block_count
    tick_count = unit_count + section_count - 1
    gain_row = norm_gain[0]
    w_joined = jnp.concatenate([w_query[0], w_key[0], w_value[0]], axis=1)
    w_down = w_out[0]
    query_cols = w_query.shape[2]
    key_cols = w_key.shape[2]
    local_heads = query_cols // HD
    kv_index = lane_index * local_heads // (HEADS // KV_HEADS)
    score_scale = 1.0 / math.sqrt(HD)
    offsets = jnp.arange(block_len, dtype=jnp.int32)
    key_positions = jnp.arange(seq_len, dtype=jnp.int32)
    incoming = jnp.zeros((shard_rows, model_width), jnp.bfloat16)
    key_cache = jnp.zeros((micro_count, seq_len, HD), jnp.bfloat16)
    value_cache = jnp.zeros((micro_count, seq_len, HD), jnp.bfloat16)
    stored = jnp.zeros((micro_count, block_count, shard_rows, model_width), jnp.bfloat16)

    def attend(projected, batch_index, block_index, key_cache, value_cache):
        queries = projected[:, :query_cols].reshape(block_len, local_heads, HD)
        key_value = projected[:, query_cols:].astype(jnp.bfloat16)
        gathered = lax.all_gather(key_value, "tensor", axis=1, tiled=True)
        gathered = gathered.reshape(block_len, lane_count, 2, key_cols)
        keys_all = gathered[:, :, 0, :].reshape(block_len, HD, KV_HEADS)
        values_all = gathered[:, :, 1, :].reshape(block_len, HD, KV_HEADS)
        key_new = lax.dynamic_index_in_dim(keys_all, kv_index, 2, keepdims=False)
        value_new = lax.dynamic_index_in_dim(values_all, kv_index, 2, keepdims=False)
        positions = block_index * block_len + offsets
        queries = rotate(queries, positions).astype(jnp.bfloat16)
        key_new = rotate(key_new.astype(jnp.float32)[:, None, :], positions)[:, 0, :].astype(
            jnp.bfloat16
        )
        key_cache = lax.dynamic_update_slice(
            key_cache, key_new[None], (batch_index, block_index * block_len, 0)
        )
        value_cache = lax.dynamic_update_slice(
            value_cache, value_new[None], (batch_index, block_index * block_len, 0)
        )
        key_rows = lax.dynamic_index_in_dim(key_cache, batch_index, 0, keepdims=False)
        value_rows = lax.dynamic_index_in_dim(value_cache, batch_index, 0, keepdims=False)
        scores = (
            jnp.einsum("qhd,kd->hqk", queries, key_rows, preferred_element_type=jnp.float32)
            * score_scale
        )
        visible = key_positions[None, :] <= positions[:, None]
        weights = jnp.where(visible[None], jnp.exp(scores), 0.0)
        weights = (weights / jnp.sum(weights, axis=-1, keepdims=True)).astype(jnp.bfloat16)
        context = jnp.einsum("hqk,kd->qhd", weights, value_rows, preferred_element_type=jnp.float32)
        context = context.astype(jnp.bfloat16).reshape(block_len, query_cols)
        reduced = lax.psum_scatter(
            jnp.dot(context, w_down, preferred_element_type=jnp.float32).astype(jnp.bfloat16),
            "tensor",
            scatter_dimension=0,
            tiled=True,
        ).astype(jnp.float32)
        return (reduced, key_cache, value_cache)

    def advance(tick_index, state_tuple):
        incoming, key_cache, value_cache, stored = state_tuple
        unit_index = tick_index - section_index
        usable = (unit_index >= 0) & (unit_index < unit_count)
        unit_index = jnp.clip(unit_index, 0, unit_count - 1)
        batch_index = unit_index // block_count
        block_index = unit_index % block_count
        arriving = lax.dynamic_slice(
            tokens, (batch_index, block_index, 0, 0), (1, 1, incoming.shape[0], model_width)
        )[0, 0]
        present = jnp.where(section_index == 0, arriving, incoming)
        projected = jnp.dot(
            lax.all_gather(normalize(present, gain_row), "tensor", axis=0, tiled=True),
            w_joined,
            preferred_element_type=jnp.float32,
        )
        reduced, key_cache, value_cache = attend(
            projected, batch_index, block_index, key_cache, value_cache
        )
        result = (present.astype(jnp.float32) + reduced).astype(jnp.bfloat16)
        previous = lax.dynamic_slice(
            stored, (batch_index, block_index, 0, 0), (1, 1, shard_rows, model_width)
        )[0, 0]
        chosen = jnp.where(usable, result, previous)
        stored = lax.dynamic_update_slice(
            stored, chosen[None, None], (batch_index, block_index, 0, 0)
        )
        incoming = shifted(result, "section", 1)
        return (incoming, key_cache, value_cache, stored)

    final_state = lax.fori_loop(0, tick_count, advance, (incoming, key_cache, value_cache, stored))
    return final_state[3][None]


PAIR = 2
MESH = pl.DeviceIdType.MESH


def layer_kernel(
    dims,
    tokens,
    gain_row,
    cos_rows,
    sin_rows,
    cos_cols,
    sin_cols,
    regroup,
    wq_hbm,
    wk_hbm,
    wv_hbm,
    wo_hbm,
    out,
    wq,
    wkv,
    wo,
    gathered,
    normed,
    squares,
    projected,
    queries,
    context,
    kv_send,
    kv_land,
    key_cache,
    value_cache,
    partial,
    pair_land,
    column_sum,
    column_land,
    finished,
    weight_sem,
    own_sem,
    rows_send,
    rows_recv,
    relay_send,
    relay_recv,
    kv_send_sem,
    kv_recv_sem,
    pair_send,
    pair_recv,
    column_send,
    column_recv,
    mixer,
    trade_send,
    trade_land,
    trade_send_sem,
    trade_recv_sem,
):
    sections, lanes, micro_count, block_count, rows, width, chunks, query_cols = dims
    columns = lanes // PAIR
    units = micro_count * block_count
    chunk = width // chunks
    block_len = rows * lanes
    seq_len = block_count * block_len
    heads = query_cols // HD
    section = lax.axis_index("section")
    lane = lax.axis_index("tensor")
    column = lane // PAIR
    side = lane % PAIR
    other = 1 - side
    partner = column * PAIR + other
    score_scale = 1.0 / math.sqrt(HD)

    def shared_weights(c):
        band = pl.ds(c * chunk, chunk)
        return [
            pltpu.make_async_copy(
                wk_hbm.at[0, band], wkv.at[band, pl.ds(0, HD)], weight_sem.at[0, c]
            ),
            pltpu.make_async_copy(
                wv_hbm.at[0, band], wkv.at[band, pl.ds(HD, HD)], weight_sem.at[1, c]
            ),
        ]

    def query_weights(c):
        band = pl.ds(c * chunk, chunk)
        return pltpu.make_async_copy(wq_hbm.at[0, band], wq.at[band], weight_sem.at[2, c])

    output_weights = pltpu.make_async_copy(wo_hbm.at[0], wo, weight_sem.at[3, 0])
    for c in range(chunks):
        for copy in shared_weights(c):
            copy.start()
        query_weights(c).start()
    output_weights.start()

    barrier = pltpu.get_barrier_semaphore()

    def greet(to_section, to_lane):
        pl.semaphore_signal(barrier, inc=1, device_id=(to_section, to_lane), device_id_type=MESH)

    for step in range(1, lanes):
        greet(section, (lane + step) % lanes)

    @pl.when(section > 0)
    def _():
        for z in range(columns):
            greet(section - 1, z * PAIR + side)

    @pl.when(section < sections - 1)
    def _():
        for z in range(columns):
            greet(section + 1, z * PAIR + side)

    neighbours = jnp.minimum(section, 1) + jnp.minimum(sections - 1 - section, 1)
    pl.semaphore_wait(barrier, lanes - 1 + columns * neighbours)

    def opposite(step):
        if step == 0:
            return column
        if step == 1:
            return column + 1 - 2 * (column % 2)
        if step == 2:
            return (column + 2) % columns
        return columns - 1 - column

    def rows_copy(source, unit, c, step, to_section):
        to_column = opposite(step)
        return pltpu.make_async_remote_copy(
            src_ref=source,
            dst_ref=gathered.at[unit, c, side, column],
            send_sem=rows_send.at[unit, c, step],
            recv_sem=rows_recv.at[unit, c, column],
            device_id=(to_section, to_column * PAIR + side),
            device_id_type=MESH,
        )

    def relay_copy(unit, c, which):
        return pltpu.make_async_remote_copy(
            src_ref=gathered.at[unit, c, which],
            dst_ref=gathered.at[unit, c, which],
            send_sem=relay_send.at[unit, c],
            recv_sem=relay_recv.at[unit, c],
            device_id=(section, partner),
            device_id_type=MESH,
        )

    def kv_copy(unit, step, landing):
        to_lane = (lane + step) % lanes
        return pltpu.make_async_remote_copy(
            src_ref=kv_send.at[unit, to_lane],
            dst_ref=kv_land.at[unit, landing],
            send_sem=kv_send_sem.at[unit, step],
            recv_sem=kv_recv_sem.at[unit, step],
            device_id=(section, to_lane),
            device_id_type=MESH,
        )

    def pair_copy(unit, c):
        return pltpu.make_async_remote_copy(
            src_ref=partial.at[unit, c, other],
            dst_ref=pair_land.at[unit, c],
            send_sem=pair_send.at[unit, c],
            recv_sem=pair_recv.at[unit, c],
            device_id=(section, partner),
            device_id_type=MESH,
        )

    def column_copy(unit, c, step):
        to_column = opposite(step)
        return pltpu.make_async_remote_copy(
            src_ref=column_sum.at[unit, c, to_column],
            dst_ref=column_land.at[unit, c, step],
            send_sem=column_send.at[unit, c, step],
            recv_sem=column_recv.at[unit, c, step],
            device_id=(section, to_column * PAIR + side),
            device_id_type=MESH,
        )

    def trade_copy(step, landing):
        to_lane = (lane + step) % lanes
        return pltpu.make_async_remote_copy(
            src_ref=trade_send.at[to_lane],
            dst_ref=trade_land.at[:, landing],
            send_sem=trade_send_sem.at[step],
            recv_sem=trade_recv_sem.at[step],
            device_id=(section, to_lane),
            device_id_type=MESH,
        )

    def token_rows(unit, c):
        return tokens.at[unit // block_count, unit % block_count, :, pl.ds(c * chunk, chunk)]

    @pl.when(section == 0)
    def _():
        @pl.loop(0, units)
        def _(unit):
            for c in range(chunks):
                for step in reversed(range(1, columns)):
                    rows_copy(token_rows(unit, c), unit, c, step, section).start()
                pltpu.make_async_copy(
                    token_rows(unit, c),
                    gathered.at[unit, c, side, column],
                    own_sem.at[unit, c],
                ).start()

    key_cache[...] = jnp.zeros_like(key_cache)
    value_cache[...] = jnp.zeros_like(value_cache)

    trades = section == TRADER
    mixer[...] = regroup[...]

    @pl.when(trades)
    def _():
        for c in range(chunks):
            for copy in shared_weights(c):
                copy.wait()

        @pl.loop(0, width // PIECE)
        def _(part):
            band = pl.ds(pl.multiple_of(part * PIECE, PIECE), PIECE)
            for i in range(2):
                turned = lax.dot_general(
                    regroup[...],
                    wkv[band, pl.ds(i * HD, HD)],
                    (((1,), (1,)), ((), ())),
                    preferred_element_type=jnp.float32,
                ).astype(jnp.bfloat16)
                trade_send[:, i, :, band] = turned.reshape(lanes, HD // lanes, PIECE)

        for step in range(1, lanes):
            trade_copy(step, lane).start()
        trade_land[:, lane] = trade_send[lane]
        for step in range(1, lanes):
            trade_copy(step, (lane + lanes - step) % lanes).wait_recv()

        line = lax.broadcasted_iota(jnp.int32, (HD, HD), 0)
        entry = lax.broadcasted_iota(jnp.int32, (HD, HD), 1)
        mixer[...] = jnp.where(line == entry, 1.0, 0.0).astype(jnp.bfloat16)

        @pl.loop(0, width // PIECE)
        def _(part):
            band = pl.ds(pl.multiple_of(part * PIECE, PIECE), PIECE)
            for i in range(2):
                wkv[band, pl.ds(i * HD, HD)] = lax.dot_general(
                    trade_land[i, :, :, band].reshape(HD, PIECE),
                    mixer[...],
                    (((0,), (0,)), ((), ())),
                    preferred_element_type=jnp.float32,
                ).astype(jnp.bfloat16)

        for step in range(1, lanes):
            trade_copy(step, lane).wait_send()

    def receive(unit, c):
        for step in range(1, columns):
            from_column = (column + step) % columns
            pltpu.make_async_remote_copy(
                src_ref=gathered.at[unit, c, side, from_column],
                dst_ref=gathered.at[unit, c, side, from_column],
                send_sem=rows_send.at[unit, c, step],
                recv_sem=rows_recv.at[unit, c, from_column],
                device_id=(section, partner),
                device_id_type=MESH,
            ).wait_recv()

        @pl.when(section == 0)
        def _():
            pltpu.make_async_copy(
                token_rows(unit, c),
                gathered.at[unit, c, side, column],
                own_sem.at[unit, c],
            ).wait()

        @pl.when(section > 0)
        def _():
            rows_copy(finished.at[unit, c], unit, c, 0, section - 1).wait_recv()

        relay_copy(unit, c, side).start()

    def absorb(unit, c):
        relay_copy(unit, c, other).wait_recv()
        cols = pl.ds(c * chunk, chunk)
        gain = gain_row[:, cols].astype(jnp.float32)
        for z in range(columns):
            band = slice(z * PAIR * rows, (z + 1) * PAIR * rows)
            x = jnp.concatenate(
                [gathered[unit, c, i, z].astype(jnp.float32) for i in range(PAIR)], axis=0
            )
            square = jnp.sum(x * x, axis=-1, keepdims=True)
            if c == 0:
                squares[band, :] = jnp.broadcast_to(square, (PAIR * rows, HD))
            else:
                squares[band, :] += square
            normed[band, :] = (x * gain).astype(jnp.bfloat16)
        product = jnp.dot(normed[...], wkv[cols, :], preferred_element_type=jnp.float32)
        if c == 0:
            projected[:, pl.ds(query_cols, 2 * HD)] = product
        else:
            projected[:, pl.ds(query_cols, 2 * HD)] += product

    def absorb_queries(c):
        @pl.loop(0, query_cols // SPAN)
        def _(part):
            place = pl.ds(pl.multiple_of(part * SPAN, SPAN), SPAN)
            product = jnp.dot(
                normed[...],
                wq[pl.ds(c * chunk, chunk), place],
                preferred_element_type=jnp.float32,
            )
            if c == 0:
                projected[:, place] = product
            else:
                projected[:, place] += product

    def row_factor():
        return lax.rsqrt(squares[:, :1] * (1.0 / width) + EPSILON)

    def share_keys(unit):
        key_value = projected[:, pl.ds(query_cols, 2 * HD)] * row_factor()
        stacked = jnp.concatenate([key_value[:, :HD], key_value[:, HD:]], axis=0)
        turned = lax.dot_general(
            mixer[...],
            stacked.astype(jnp.bfloat16),
            (((1,), (1,)), ((), ())),
            preferred_element_type=jnp.float32,
        ).astype(jnp.bfloat16)
        turned = turned.reshape(lanes, HD // lanes, 2 * block_len)

        @pl.when(trades)
        def _():
            kv_land[unit] = turned

        @pl.when(section != TRADER)
        def _():
            kv_send[unit] = turned
            for step in range(1, lanes):
                kv_copy(unit, step, lane).start()
            kv_land[unit, lane] = kv_send[unit, lane]

    def attend(unit):
        micro = unit // block_count
        block = unit % block_count
        factor = row_factor()
        cosine = cos_rows[block]
        sine = sin_rows[block]
        for h in range(heads):
            head = projected[:, pl.ds(h * HD, HD)] * factor
            turned_head = head * cosine + pltpu.roll(head, HD // 2, 1) * sine
            queries[pl.ds(h * block_len, block_len), :] = turned_head.astype(jnp.bfloat16)

        @pl.when(section != TRADER)
        def _():
            for step in range(1, lanes):
                kv_copy(unit, step, (lane + lanes - step) % lanes).wait_recv()

        landed = kv_land[unit].reshape(HD, 2 * block_len).astype(jnp.float32)
        lower = landed[: HD // 2]
        upper = landed[HD // 2 :]
        cosine_col = cos_cols[block]
        sine_col = sin_cols[block]
        rotated = jnp.concatenate(
            [lower * cosine_col - upper * sine_col, upper * cosine_col + lower * sine_col], axis=0
        )
        place = lax.broadcasted_iota(jnp.int32, (HD, seq_len), 1)
        fresh = place // block_len == block
        swapped = jnp.where(block == 0, rotated, pltpu.roll(rotated, block_len, 1))
        keys = jnp.where(fresh, swapped, key_cache[micro].astype(jnp.float32)).astype(jnp.bfloat16)
        key_cache[micro] = keys
        swapped = jnp.where(block == 0, pltpu.roll(landed, block_len, 1), landed)
        values = jnp.where(fresh, swapped, value_cache[micro].astype(jnp.float32)).astype(
            jnp.bfloat16
        )
        value_cache[micro] = values

        stack = heads * block_len
        position = (
            lax.broadcasted_iota(jnp.int32, (stack, seq_len), 0) % block_len + block * block_len
        )
        key_position = lax.broadcasted_iota(jnp.int32, (stack, seq_len), 1)
        scores = jnp.dot(queries[...], keys, preferred_element_type=jnp.float32) * score_scale
        piece = jnp.where(key_position <= position, jnp.exp(scores), 0.0)
        denominator = jnp.sum(piece, axis=-1, keepdims=True)
        result = lax.dot_general(
            (piece / denominator).astype(jnp.bfloat16),
            values,
            (((1,), (1,)), ((), ())),
            preferred_element_type=jnp.float32,
        ).astype(jnp.bfloat16)
        for h in range(heads):
            context[:, pl.ds(h * HD, HD)] = result[h * block_len : (h + 1) * block_len]

    def down(unit, c):
        tile = TILE

        @pl.loop(0, chunk // tile)
        def _(n):
            start = pl.multiple_of(n * tile, tile)
            product = jnp.dot(
                context[...],
                wo[:, pl.ds(pl.multiple_of(c * chunk + start, tile), tile)],
                preferred_element_type=jnp.float32,
            )
            blocks = product.reshape(columns, PAIR, rows, tile).astype(jnp.bfloat16)
            for i in range(PAIR):
                partial[unit, c, i, :, :, pl.ds(start, tile)] = blocks[:, i]

        pair_copy(unit, c).start()

    def add_pair(unit, c):
        pair_copy(unit, c).wait_recv()
        for z in range(columns):
            column_sum[unit, c, z] = (
                partial[unit, c, side, z].astype(jnp.float32)
                + pair_land[unit, c, z].astype(jnp.float32)
            ).astype(jnp.bfloat16)
        for step in reversed(range(1, columns)):
            column_copy(unit, c, step).start()

    def finish(unit, c):
        total = gathered[unit, c, side, column].astype(jnp.float32)
        total = total + column_sum[unit, c, column].astype(jnp.float32)
        for step in range(1, columns):
            column_copy(unit, c, step).wait_recv()
            total = total + column_land[unit, c, step].astype(jnp.float32)
        result = total.astype(jnp.bfloat16)
        finished[unit, c] = result
        out[0, unit // block_count, unit % block_count, :, pl.ds(c * chunk, chunk)] = result

        @pl.when(section < sections - 1)
        def _():
            for step in reversed(range(columns)):
                rows_copy(finished.at[unit, c], unit, c, step, section + 1).start()

    @pl.when(section == 0)
    def _():
        for c in range(chunks):
            receive(0, c)

    @pl.loop(0, units + 1)
    def _(turn):
        older = turn - 1

        def step_of(name, c):
            if name == "D":
                down(older, c)
            elif name == "P":
                add_pair(older, c)
            elif name == "F":
                finish(older, c)
            elif name == "R":
                @pl.when(section > 0)
                def _():
                    receive(turn, c)
            elif name == "E":
                @pl.when((section == 0) & (turn < units - 1))
                def _():
                    receive(turn + 1, c)
            elif name == "A":

                @pl.when(turn == 0)
                def _():
                    query_weights(c).wait()

                @pl.when((turn == 0) & (section != TRADER))
                def _():
                    for copy in shared_weights(c):
                        copy.wait()

                absorb(turn, c)
                if c < chunks - 1:
                    absorb_queries(c)
            elif name == "K":
                share_keys(turn)
                absorb_queries(chunks - 1)
            elif name == "T":
                attend(turn)

                @pl.when(turn == 0)
                def _():
                    output_weights.wait()

        groups = []
        for word in SCHEDULE:
            late = word[0] in "DPF"
            if not groups or groups[-1][0] != late:
                groups.append((late, []))
            groups[-1][1].append((word[0], int(word[1:] or 0)))
        for late, members in groups:
            @pl.when((turn > 0) if late else (turn < units))
            def _():
                for name, c in members:
                    step_of(name, c)

    @pl.loop(0, units)
    def _(unit):
        for c in range(chunks):
            relay_copy(unit, c, side).wait_send()
            pair_copy(unit, c).wait_send()
            for step in range(1, columns):
                column_copy(unit, c, step).wait_send()

        @pl.when(section != TRADER)
        def _():
            for step in range(1, lanes):
                kv_copy(unit, step, lane).wait_send()

    @pl.when(section == 0)
    def _():
        @pl.loop(0, units)
        def _(unit):
            for c in range(chunks):
                for step in range(1, columns):
                    rows_copy(token_rows(unit, c), unit, c, step, section).wait_send()

    @pl.when(section < sections - 1)
    def _():
        @pl.loop(0, units)
        def _(unit):
            for c in range(chunks):
                for step in range(columns):
                    rows_copy(finished.at[unit, c], unit, c, step, section + 1).wait_send()


def kernel_body(tokens, norm_gain, w_query, w_key, w_value, w_out):
    sections = lax.axis_size("section")
    lanes = lax.axis_size("tensor")
    micro_count, block_count, rows, width = tokens.shape
    query_cols = w_query.shape[2]
    block_len = rows * lanes
    seq_len = block_count * block_len
    units = micro_count * block_count
    columns = lanes // PAIR
    chunks = CHUNKS
    chunk = width // chunks
    half = HD // 2
    frequency = np.power(
        np.float32(ROPE_BASE), -(np.arange(half, dtype=np.float32) * np.float32(2.0)) / np.float32(HD)
    )
    angles = np.arange(seq_len, dtype=np.float32)[:, None] * frequency[None, :]
    cosine, sine = np.cos(angles), np.sin(angles)
    cos_rows = np.concatenate([cosine, cosine], axis=1).reshape(block_count, block_len, HD)
    sin_rows = np.concatenate([-sine, sine], axis=1).reshape(block_count, block_len, HD)

    def by_column(table):
        table = np.swapaxes(table.reshape(block_count, block_len, half), 1, 2)
        return np.concatenate([table, table], axis=2)

    entries = HD // KV_HEADS
    target = np.arange(HD)
    source = (target % entries) * KV_HEADS + target // entries
    regroup = (source[:, None] == np.arange(HD)[None, :]).astype(jnp.bfloat16)
    dims = (sections, lanes, micro_count, block_count, rows, width, chunks, query_cols)
    vmem = pl.BlockSpec(memory_space=pltpu.VMEM)
    hbm = pl.BlockSpec(memory_space=pl.ANY)
    dma = pltpu.SemaphoreType.DMA
    bf16 = jnp.bfloat16
    return pl.pallas_call(
        functools.partial(layer_kernel, dims),
        out_shape=jax.ShapeDtypeStruct((1,) + tokens.shape, bf16),
        in_specs=[vmem] * 7 + [hbm] * 4,
        out_specs=vmem,
        scratch_shapes=[
            pltpu.VMEM((width, query_cols), bf16),
            pltpu.VMEM((width, 2 * HD), bf16),
            pltpu.VMEM((query_cols, width), bf16),
            pltpu.VMEM((units, chunks, PAIR, columns, rows, chunk), bf16),
            pltpu.VMEM((block_len, chunk), bf16),
            pltpu.VMEM((block_len, HD), jnp.float32),
            pltpu.VMEM((block_len, query_cols + 2 * HD), jnp.float32),
            pltpu.VMEM((query_cols // HD * block_len, HD), bf16),
            pltpu.VMEM((block_len, query_cols), bf16),
            pltpu.VMEM((units, lanes, HD // lanes, 2 * block_len), bf16),
            pltpu.VMEM((units, lanes, HD // lanes, 2 * block_len), bf16),
            pltpu.VMEM((micro_count, HD, seq_len), bf16),
            pltpu.VMEM((micro_count, HD, seq_len), bf16),
            pltpu.VMEM((units, chunks, PAIR, columns, rows, chunk), bf16),
            pltpu.VMEM((units, chunks, columns, rows, chunk), bf16),
            pltpu.VMEM((units, chunks, columns, rows, chunk), bf16),
            pltpu.VMEM((units, chunks, columns, rows, chunk), bf16),
            pltpu.VMEM((units, chunks, rows, chunk), bf16),
            dma((4, chunks)),
            dma((units, chunks)),
            dma((units, chunks, columns)),
            dma((units, chunks, columns)),
            dma((units, chunks)),
            dma((units, chunks)),
            dma((units, lanes)),
            dma((units, lanes)),
            dma((units, chunks)),
            dma((units, chunks)),
            dma((units, chunks, columns)),
            dma((units, chunks, columns)),
            pltpu.VMEM((HD, HD), bf16),
            pltpu.VMEM((lanes, 2, HD // lanes, width), bf16),
            pltpu.VMEM((2, lanes, HD // lanes, width), bf16),
            dma((lanes,)),
            dma((lanes,)),
        ],
        compiler_params=pltpu.CompilerParams(
            collective_id=0, has_side_effects=True, vmem_limit_bytes=67043328
        ),
    )(
        tokens,
        norm_gain,
        jnp.asarray(cos_rows),
        jnp.asarray(sin_rows),
        jnp.asarray(by_column(cosine)),
        jnp.asarray(by_column(sine)),
        jnp.asarray(regroup),
        w_query,
        w_key,
        w_value,
        w_out,
    )


CHUNKS = 4
SPAN = 1024
TILE = 2048
TRADER = 2
PIECE = 1024
SCHEDULE = ("D0", "D1", "D2", "D3", "P0", "P1", "E0", "E1", "R0", "P2", "R1", "P3", "R2", "E2", "E3", "F0", "R3", "A0", "F1", "A1", "F2", "A2", "F3", "A3", "K", "T")


def body(tokens, norm_gain, w_query, w_key, w_value, w_out):
    lanes = lax.axis_size("tensor")
    fits = (
        lanes == KV_HEADS
        and w_key.shape[2] == HD
        and w_query.shape[2] == HEADS // KV_HEADS * HD
        and tokens.shape[2] == 8
        and tokens.shape[2] * lanes * 2 == HD
        and tokens.shape[1] == 2
        and lanes == 4 * PAIR
        and tokens.shape[3] % (CHUNKS * TILE) == 0
        and w_query.shape[2] % SPAN == 0
        and tokens.shape[3] % PIECE == 0
    )
    chosen = kernel_body if fits else general_body
    return chosen(tokens, norm_gain, w_query, w_key, w_value, w_out)


def solution(mesh):
    return jax.shard_map(
        body,
        mesh=mesh,
        in_specs=(
            P(None, None, "tensor", None),
            P("section", None),
            P("section", None, "tensor"),
            P("section", None, "tensor"),
            P("section", None, "tensor"),
            P("section", "tensor", None),
        ),
        out_specs=P("section", None, None, "tensor", None),
        check_vma=False,
    )
```
